256 devices in a mesh: seq: 64 (over z, y, core), head: 4 (over x).
Axes of the slice: x: 4, y: 4, z: 8, core: 2. Of those that a mesh axis runs over, the one named last changes fastest.
Arguments:
- queries: bfloat16 [2, 4096, 2048], P(None, 'seq', 'head'), may hold values from -6 to 6
- keys: bfloat16 [2, 4096, 2048], P(None, 'seq', 'head'), may hold values from -6 to 6
- values: bfloat16 [2, 4096, 2048], P(None, 'seq', 'head'), may hold values from -6 to 6
- out_weight: bfloat16 [2048, 4096], P('head'), may hold values from -0.125 to 0.125
- upstream: bfloat16 [2, 4096, 4096], P(None, 'seq', 'head'), may hold values from -16 to 16
Outputs:
- output: bfloat16 [2, 4096, 4096], P(None, 'seq', 'head')
- query_grad: bfloat16 [2, 4096, 2048], P(None, 'seq', 'head')
- key_grad: bfloat16 [2, 4096, 2048], P(None, 'seq', 'head')
- value_grad: bfloat16 [2, 4096, 2048], P(None, 'seq', 'head')
- weight_grad: float32 [2048, 4096], P('head', 'seq')
The draws below stay inside these ranges and needn't reach their ends.
All inputs are finite; a program needn't handle non-finite values.
Results may differ from the reference program's by a relative error of at most 0.01405.
Values may be sent and summed in bfloat16 or wider, within the bound.
A program may use at most 128 MiB of HBM per device.

```python
import jax
import jax.numpy as jnp
from jax import lax

D = 4096
HEADS = 16
HEAD_DIM = 128
SPAN = 64
HD = 2048
HALF = 4096
N_SEQ = 64


def raised(entries, key, source, target, shards_of, factor):
    def block_of(dim):
        return (jnp.arange(entries.shape[dim]) // (entries.shape[dim] // shards_of)).reshape((-1,) + (1,) * (entries.ndim - 1 - dim))

    near = jax.random.permutation(key, shards_of)[block_of(target)]
    second = (block_of(target) + shards_of // 2) % shards_of
    return jnp.where((block_of(source) == near) | (block_of(source) == second), factor * entries, entries)


def block_scale(stream_key, dims, cuts, low, largest):
    factor_of, own = 1.0, jax.random.fold_in(stream_key, 6)
    for dim, blocks in cuts:
        steps = jnp.exp(jax.random.uniform(jax.random.fold_in(own, dim), (blocks,), jnp.float32, low / len(cuts), largest / len(cuts)))
        factor_of = factor_of * jnp.repeat(steps, dims[dim] // blocks).reshape([-1 if axis == dim else 1 for axis in range(len(dims))])
    return factor_of


def centred(own_key, shape, scale, bound, shards=(), kind=jnp.bfloat16):
    entries = jax.random.normal(own_key, shape, jnp.float32) * scale
    if len(shards) > 0:
        entries = block_scale(own_key, shape, shards, -0.22, 0.18) * entries
    return jnp.clip(entries, min=-bound, max=bound).astype(kind)


def heavy_noise(stream_key, dims, scale, reach, cuts, heavy, dtype=jnp.bfloat16):
    drawn = scale * jax.random.normal(stream_key, dims, jnp.float32)
    if cuts:
        drawn = drawn * block_scale(stream_key, dims, cuts, -0.22, 0.18)
    return jnp.clip(raised(drawn, jax.random.fold_in(stream_key, 3), *heavy), -reach, reach).astype(dtype)


def setup_inputs(seed: int = 0) -> dict:
    splits = jax.random.split(jax.random.key(seed), 6)
    return {
        "queries": centred(splits[0], (2, HALF, HD), 1.0, 6.0, ((1, 64), (2, 4))),
        "keys": centred(splits[1], (2, HALF, HD), 1.0, 6.0, ((1, 64), (2, 4))),
        "values": centred(splits[2], (2, HALF, HD), 1.0, 6.0, ((1, 64), (2, 4))),
        "out_weight": centred(splits[3], (HD, D), HD ** -0.5, 0.125, ((0, 4),)),
        "upstream": heavy_noise(splits[4], (2, HALF, D), 1.0, 16.0, ((1, 64), (2, 4)), (1, 2, 64, 4.0)),
    }


eps = 1e-06

def natural(arr):
    width = arr.shape[-1]
    blocks = arr[1].reshape(N_SEQ, SPAN, width)[::-1].reshape(N_SEQ * SPAN, width)
    return jnp.concatenate([arr[0], blocks], axis=0)

def to_pairs(arr):
    half = arr.shape[0] // 2
    width = arr.shape[-1]
    second = arr[half:].reshape(N_SEQ, SPAN, width)[::-1].reshape(half, width)
    return jnp.stack([arr[:half], second])

def lower_mask():
    rows = lax.broadcasted_iota(jnp.int32, (SPAN, SPAN), 0)
    cols = lax.broadcasted_iota(jnp.int32, (SPAN, SPAN), 1)
    return rows >= cols

def head_states(query, key, value):
    qf = query.astype(jnp.float32)
    kf = key.astype(jnp.float32)
    vf = value.astype(jnp.float32)
    kv_terms = jnp.einsum('ncd,nce->nde', kf, vf)
    summed = jnp.cumsum(kv_terms, axis=0)[:-1]
    states = jnp.concatenate([jnp.zeros_like(kv_terms[:1]), summed], axis=0).astype(jnp.bfloat16)
    weights = jnp.where(lower_mask(), jnp.einsum('ntd,nsd->nts', qf, kf), 0.0).astype(jnp.bfloat16)
    return (qf, kf, vf, states, weights)

def forward_head(operands):
    query, key, value = operands
    qf, kf, vf, states, weights = head_states(query, key, value)
    return jnp.einsum('nts,nse->nte', weights.astype(jnp.float32), vf) + jnp.einsum('ntd,nde->nte', qf, states.astype(jnp.float32))

def backward_head(operands):
    query, key, value, grad = operands
    qf, kf, vf, states, weights = head_states(query, key, value)
    gf = grad.astype(jnp.float32)
    qg_terms = jnp.einsum('ncd,nce->nde', qf, gf)
    reverse_sum = jnp.cumsum(qg_terms[::-1], axis=0)[::-1]
    later = jnp.concatenate([reverse_sum[1:], jnp.zeros_like(qg_terms[:1])], axis=0).astype(jnp.bfloat16)
    laterf = later.astype(jnp.float32)
    diffs = jnp.where(lower_mask(), jnp.einsum('nte,nse->nts', gf, vf), 0.0).astype(jnp.bfloat16)
    diffsf = diffs.astype(jnp.float32)
    query_grad = jnp.einsum('nts,nsd->ntd', diffsf, kf) + jnp.einsum('nte,nde->ntd', gf, states.astype(jnp.float32))
    key_grad = jnp.einsum('nts,ntd->nsd', diffsf, qf) + jnp.einsum('nse,nde->nsd', vf, laterf)
    value_grad = jnp.einsum('nts,nte->nse', weights.astype(jnp.float32), gf) + jnp.einsum('nsd,nde->nse', kf, laterf)
    return (query_grad.astype(jnp.bfloat16), key_grad.astype(jnp.bfloat16), value_grad.astype(jnp.bfloat16))

def reference(queries, keys, values, out_weight, upstream):
    blocks = 2 * N_SEQ

    def by_head(arr):
        return natural(arr).reshape(blocks, SPAN, HEADS, HEAD_DIM).transpose(2, 0, 1, 3)

    def by_rows(arr):
        return to_pairs(arr.transpose(1, 2, 0, 3).reshape(blocks * SPAN, HEADS * HEAD_DIM))
    query_heads = by_head(queries)
    key_heads = by_head(keys)
    value_heads = by_head(values)
    attended = lax.map(forward_head, (query_heads, key_heads, value_heads))
    scale = jnp.sqrt(lax.optimization_barrier(jnp.mean(attended * attended, axis=-1, keepdims=True)) + eps)
    normed = attended / scale
    hidden = normed.astype(jnp.bfloat16).transpose(1, 2, 0, 3).reshape(blocks * SPAN, HEADS * HEAD_DIM)
    output = jnp.dot(hidden, out_weight, preferred_element_type=jnp.float32).astype(jnp.bfloat16)
    full_up = natural(upstream)
    hidden_grad = jnp.dot(full_up, out_weight.T, preferred_element_type=jnp.float32)
    weight_grad = jnp.dot(hidden.T, full_up, preferred_element_type=jnp.float32)
    grad_heads = hidden_grad.reshape(blocks, SPAN, HEADS, HEAD_DIM).transpose(2, 0, 1, 3)
    inner = lax.optimization_barrier(jnp.mean(grad_heads * normed, axis=-1, keepdims=True))
    attn_grad = ((grad_heads - normed * inner) / scale).astype(jnp.bfloat16)
    query_grad, key_grad, value_grad = lax.map(backward_head, (query_heads, key_heads, value_heads, attn_grad))
    return (to_pairs(output), by_rows(query_grad), by_rows(key_grad), by_rows(value_grad), weight_grad)
```

```python
import functools

import jax
import jax.numpy as jnp
from jax import lax
from jax.experimental import pallas as pl
from jax.experimental.pallas import tpu as pltpu
from jax.sharding import PartitionSpec as P

MESH = pl.DeviceIdType.MESH
SPAN = 64
HEAD_DIM = 128
EPS = 1e-06
NZ = 8
NY = 4
F32 = jnp.float32
BF16 = jnp.bfloat16


def nn(a, b):
    return lax.dot_general(a, b, (((1,), (0,)), ((), ())), preferred_element_type=F32)


def nt(a, b):
    return lax.dot_general(a, b, (((1,), (1,)), ((), ())), preferred_element_type=F32)


def tn(a, b):
    return lax.dot_general(a, b, (((0,), (0,)), ((), ())), preferred_element_type=F32)


def kernel(
    nz, ny, nx,
    q_hbm, k_hbm, v_hbm, w_hbm, up_hbm,
    out_ref, qg_ref, kg_ref, vg_ref, wg_ref,
    q, k, v, w, upf, uprow,
    ssend, srow, zsend, zbuf, tsend, trow,
    wts, att, normed, scale, hidden, hg, ag, qacc, kacc, vacc,
    hsend, hrow, wsend, wrow, wmine, wother,
    osend, orecv, oown,
    in_sem, w_sem, ups_sem, upr_sem, urs_sem, urr_sem, pfs_sem, pfr_sem,
    s1s, s1r, s2s, s2r, s3s, s3r, hs_sem, hr_sem, ws_sem, wr_sem, xs_sem, xr_sem,
    os_sem, or_sem,
):
    rows = 2 * ny
    heads = q.shape[1] // HEAD_DIM
    width = q.shape[1]
    dx = up_hbm.shape[1]
    sl = width // rows
    pieces = HEAD_DIM // sl
    zcols = ny * 128
    zper = dx // zcols
    half = width // 2

    s_me = lax.axis_index("seq")
    x_me = lax.axis_index("head")
    z_me = s_me // rows
    r_me = s_me % rows
    y_me = r_me // 2
    c_me = r_me % 2

    def at_row(r):
        return (z_me * rows + r, x_me)

    def at_z(z):
        return (z * rows + r_me, x_me)

    def at_x(x):
        return (s_me, x)

    def remote(src, dst, send, recv, device):
        return pltpu.make_async_remote_copy(
            src_ref=src, dst_ref=dst, send_sem=send, recv_sem=recv,
            device_id=device, device_id_type=MESH,
        )

    kv_in = [
        pltpu.make_async_copy(src, dst, in_sem.at[i])
        for i, (src, dst) in enumerate(((k_hbm, k), (v_hbm, v), (q_hbm, q)))
    ]
    for copy in kv_in:
        copy.start()
    up_own = pltpu.make_async_copy(up_hbm, upf.at[x_me], in_sem.at[3])
    up_own.start()
    w_in = [
        pltpu.make_async_copy(w_hbm.at[:, pl.ds(j * dx, dx)], w.at[j], w_sem.at[j])
        for j in range(nx)
    ]
    for copy in w_in:
        copy.start()

    barrier = pltpu.get_barrier_semaphore()
    for j in range(1, rows):
        pl.semaphore_signal(barrier, inc=1, device_id=at_row((r_me + j) % rows), device_id_type=MESH)
    for j in range(1, nz):
        pl.semaphore_signal(barrier, inc=1, device_id=at_z((z_me + j) % nz), device_id_type=MESH)
    for j in range(1, nx):
        pl.semaphore_signal(barrier, inc=1, device_id=at_x((x_me + j) % nx), device_id_type=MESH)
    pl.semaphore_wait(barrier, rows + nz + nx - 3)

    waits = []

    up_copies = {}
    for j in range(1, nx):
        copy = remote(up_hbm, upf.at[x_me], ups_sem.at[j], upr_sem.at[j], at_x((x_me + j) % nx))
        copy.start()
        up_copies[j] = copy
        waits.append(copy)

    def lanes(h):
        return slice(h * HEAD_DIM, (h + 1) * HEAD_DIM)

    def span(p):
        return slice(p * SPAN, (p + 1) * SPAN)

    def exchange_slices(which, send, into, ssem, rsem):
        copies = []
        for j in range(1, rows):
            peer = (r_me + j) % rows
            copy = remote(
                send.at[which, peer], into.at[which, r_me],
                ssem.at[which, j], rsem.at[which, j], at_row(peer),
            )
            copy.start()
            copies.append(copy)
            waits.append(copy)
        into[which, r_me] = send[which, r_me]
        return copies

    def put_terms(which, p, h, term):
        term = term.astype(BF16)
        for i in range(pieces):
            ssend[which, h * pieces + i, p] = term[i * sl:(i + 1) * sl]

    def row_sums(which, first, copies):
        for copy in copies:
            copy.wait_recv()
        low = srow[which, 0, first].astype(F32)
        high = srow[which, 0, 1 - first].astype(F32)
        for r in range(1, rows):
            low = low + srow[which, r, first].astype(F32)
            high = high + srow[which, r, 1 - first].astype(F32)
        zsend[which, 0] = low.astype(BF16)
        zsend[which, 1] = (low + high).astype(BF16)
        zbuf[which, z_me] = low.astype(BF16)
        out = []
        for j in range(1, nz):
            copy = remote(
                zsend.at[which, (z_me + j) // nz], zbuf.at[which, z_me],
                s2s.at[which, j], s2r.at[which, j], at_z((z_me + j) % nz),
            )
            copy.start()
            out.append(copy)
            waits.append(copy)
        return out

    def prefixes(which, first, copies):
        for copy in copies:
            copy.wait_recv()
        below = jnp.zeros((sl, HEAD_DIM), F32)
        total = jnp.zeros((sl, HEAD_DIM), F32)
        for j in range(nz):
            term = zbuf[which, j].astype(F32)
            total = total + term
            below = below + jnp.where(j < z_me, term, 0.0)
        for r in range(rows):
            tsend[which, r, first] = below.astype(BF16)
            below = below + srow[which, r, first].astype(F32)
        for r in range(rows - 1, -1, -1):
            tsend[which, r, 1 - first] = total.astype(BF16)
            total = total + srow[which, r, 1 - first].astype(F32)
        return exchange_slices(which, tsend, trow, s3s, s3r)

    def state_of(which, p, h):
        return jnp.concatenate(
            [trow[which, h * pieces + i, p] for i in range(pieces)], axis=0
        )

    kv_in[0].wait()
    kv_in[1].wait()
    for h in range(heads):
        for p in range(2):
            put_terms(0, p, h, tn(k[span(p), lanes(h)], v[span(p), lanes(h)]))
    step1 = exchange_slices(0, ssend, srow, s1s, s1r)

    kv_in[2].wait()
    row_i = lax.broadcasted_iota(jnp.int32, (2 * SPAN, 2 * SPAN), 0)
    col_i = lax.broadcasted_iota(jnp.int32, (2 * SPAN, 2 * SPAN), 1)
    mask = (row_i >= col_i) & ((row_i < SPAN) | (col_i >= SPAN))
    for h in range(heads):
        weights = jnp.where(mask, nt(q[:, lanes(h)], k[:, lanes(h)]), 0.0).astype(BF16)
        wts[h] = weights
        att[:, lanes(h)] = nn(weights, v[:, lanes(h)])

    step2 = row_sums(0, 0, step1)

    row_copies = {}

    def take_slot(j):
        slot = (x_me - j + nx) % nx
        if j == 0:
            up_own.wait()
        else:
            up_copies[j].wait_recv()
        for b in range(zper):
            for m in range(1, ny):
                peer_y = (y_me + m) % ny
                copy = remote(
                    upf.at[slot, :, pl.ds(pl.multiple_of(b * zcols + peer_y * 128, 128), 128)],
                    uprow.at[r_me, :, pl.ds(pl.multiple_of((slot * zper + b) * 128, 128), 128)],
                    urs_sem.at[m, j * zper + b], urr_sem.at[m, j * zper + b],
                    at_row(peer_y * 2 + c_me),
                )
                copy.start()
                row_copies[(m, j, b)] = copy
                waits.append(copy)
        for b in range(zper):
            uprow[r_me, :, pl.ds(pl.multiple_of((slot * zper + b) * 128, 128), 128)] = upf[
                slot, :, pl.ds(pl.multiple_of(b * zcols + y_me * 128, 128), 128)
            ]
        part = nt(upf[slot], w[slot])
        hg[...] = part if j == 0 else hg[...] + part

    for copy in w_in:
        copy.wait()
    order = [0, 1] + ([nx - 1] if nx > 2 else []) + list(range(2, nx - 1))
    for j in order[:3]:
        take_slot(j)

    step3 = prefixes(0, 0, step2)
    for j in order[3:]:
        take_slot(j)
    for copy in step3:
        copy.wait_recv()

    for h in range(heads):
        local = att[:, lanes(h)] + jnp.concatenate(
            [nn(q[span(p), lanes(h)], state_of(0, p, h)) for p in range(2)], axis=0
        )
        deviation = jnp.sqrt(jnp.mean(local * local, axis=-1, keepdims=True) + EPS)
        unit = local / deviation
        normed[:, lanes(h)] = unit
        scale[:, lanes(h)] = jnp.broadcast_to(deviation, (2 * SPAN, HEAD_DIM))
        hidden[:, lanes(h)] = unit.astype(BF16)
        hsend[lanes(h), :] = jnp.transpose(unit).astype(BF16)

    hid_copies = []
    for j in range(1, rows):
        peer = (r_me + j) % rows
        copy = remote(
            hsend.at[pl.ds(pl.multiple_of((peer % 2) * half, 128), half)], hrow.at[r_me],
            hs_sem.at[j], hr_sem.at[j], at_row(peer),
        )
        copy.start()
        hid_copies.append(copy)
        waits.append(copy)
    hrow[r_me] = hsend[pl.ds(pl.multiple_of(c_me * half, 128), half)]

    for h in range(heads):
        unit = normed[:, lanes(h)]
        grad = hg[:, lanes(h)]
        inner = jnp.mean(grad * unit, axis=-1, keepdims=True)
        attn = ((grad - unit * inner) / scale[:, lanes(h)]).astype(BF16)
        ag[:, lanes(h)] = attn
        for p in range(2):
            put_terms(1, p, h, tn(q[span(p), lanes(h)], attn[span(p)]))
    back1 = exchange_slices(1, ssend, srow, s1s, s1r)

    out_copies = []
    for j in range(1, nx):
        peer = (x_me + j) % nx
        osend[j] = nn(hidden[...], w[peer]).astype(BF16)
        copy = remote(osend.at[j], orecv.at[j], os_sem.at[j], or_sem.at[j], at_x(peer))
        copy.start()
        out_copies.append(copy)
        waits.append(copy)

    back2 = row_sums(1, 1, back1)

    part_copies = []
    for m in range(ny):
        if m > 0:
            for j in range(nx):
                for b in range(zper):
                    row_copies[(m, j, b)].wait_recv()
        slot = ((y_me - m + ny) % ny) * 2 + c_me
        copy = remote(
            uprow.at[slot], uprow.at[slot], pfs_sem.at[m], pfr_sem.at[m],
            at_row(y_me * 2 + 1 - c_me),
        )
        copy.start()
        part_copies.append(copy)
        waits.append(copy)

    oown[...] = nn(hidden[...], w[x_me])
    for h in range(heads):
        attn = ag[:, lanes(h)]
        diffs = jnp.where(mask, nt(attn, v[:, lanes(h)]), 0.0).astype(BF16)
        qacc[:, lanes(h)] = nn(diffs, k[:, lanes(h)]) + jnp.concatenate(
            [nt(attn[span(p)], state_of(0, p, h)) for p in range(2)], axis=0
        )
        kacc[:, lanes(h)] = tn(diffs, q[:, lanes(h)])
        vacc[:, lanes(h)] = tn(wts[h], attn)
    qg_ref[...] = qacc[...].astype(BF16)

    for copy in hid_copies:
        copy.wait_recv()
    for copy in part_copies:
        copy.wait_recv()

    feats = jnp.concatenate([hrow[r] for r in range(rows)], axis=1)
    group = 2 if nz % 2 == 0 else 1
    for g in range(0, nz, group):
        cols = jnp.concatenate(
            [uprow[r, :, g * 128:(g + group) * 128] for r in range(rows)], axis=0
        )
        part = nn(feats, cols).astype(BF16)
        for b in range(group):
            wsend[g + b] = part[:, b * 128:(b + 1) * 128]
    wg_copies = []
    for j in range(1, nz):
        peer = (z_me + j) % nz
        copy = remote(wsend.at[peer], wrow.at[z_me], ws_sem.at[j], wr_sem.at[j], at_z(peer))
        copy.start()
        wg_copies.append(copy)
        waits.append(copy)
    wrow[z_me] = wsend[z_me]

    back3 = prefixes(1, 1, back2)

    total = oown[...]
    for j, copy in enumerate(out_copies):
        copy.wait_recv()
        total = total + orecv[j + 1].astype(F32)
    out_ref[...] = total.astype(BF16)

    for copy in back3:
        copy.wait_recv()
    for h in range(heads):
        later = [state_of(1, p, h) for p in range(2)]
        kg_ref[:, lanes(h)] = (
            kacc[:, lanes(h)]
            + jnp.concatenate([nt(v[span(p), lanes(h)], later[p]) for p in range(2)], axis=0)
        ).astype(BF16)
        vg_ref[:, lanes(h)] = (
            vacc[:, lanes(h)]
            + jnp.concatenate([nn(k[span(p), lanes(h)], later[p]) for p in range(2)], axis=0)
        ).astype(BF16)

    for copy in wg_copies:
        copy.wait_recv()
    total = wrow[0].astype(F32)
    for j in range(1, nz):
        total = total + wrow[j].astype(F32)
    wmine[...] = total
    swap = remote(wmine, wother, xs_sem.at[0], xr_sem.at[0], at_row(y_me * 2 + 1 - c_me))
    swap.start()
    waits.append(swap)
    wg_ref[pl.ds(pl.multiple_of(c_me * half, 8), half), :] = jnp.where(
        c_me == 0, total[:, :64], total[:, 64:]
    )
    swap.wait_recv()
    total = wother[...]
    wg_ref[pl.ds(pl.multiple_of((1 - c_me) * half, 8), half), :] = jnp.where(
        c_me == 0, total[:, :64], total[:, 64:]
    )
    for copy in waits:
        copy.wait_send()


def on_device(queries, keys, values, out_weight, upstream):
    nx = lax.axis_size("head")
    nz, ny = NZ, NY
    rows = 2 * ny
    pair, length, width = queries.shape
    tokens = pair * length
    heads = width // HEAD_DIM
    dx = upstream.shape[2]
    d = out_weight.shape[1]
    sl = width // rows
    half = width // 2
    zper = dx // (ny * 128)
    flat = lambda a: a.reshape(tokens, a.shape[2])
    vmem = pltpu.VMEM
    dma = lambda *shape: pltpu.SemaphoreType.DMA(shape)
    scratch = [
        vmem((tokens, width), BF16), vmem((tokens, width), BF16), vmem((tokens, width), BF16),
        vmem((nx, width, dx), BF16),
        vmem((nx, tokens, dx), BF16),
        vmem((rows, tokens, nz * 128), BF16),
        vmem((2, rows, 2, sl, HEAD_DIM), BF16),
        vmem((2, rows, 2, sl, HEAD_DIM), BF16),
        vmem((2, 2, sl, HEAD_DIM), BF16),
        vmem((2, nz, sl, HEAD_DIM), BF16),
        vmem((2, rows, 2, sl, HEAD_DIM), BF16),
        vmem((2, rows, 2, sl, HEAD_DIM), BF16),
        vmem((heads, tokens, tokens), BF16),
        vmem((tokens, width), F32), vmem((tokens, width), F32), vmem((tokens, width), F32),
        vmem((tokens, width), BF16), vmem((tokens, width), F32), vmem((tokens, width), BF16),
        vmem((tokens, width), F32), vmem((tokens, width), F32), vmem((tokens, width), F32),
        vmem((width, tokens), BF16), vmem((rows, half, tokens), BF16),
        vmem((nz, half, 128), BF16), vmem((nz, half, 128), BF16),
        vmem((half, 128), F32), vmem((half, 128), F32),
        vmem((nx, tokens, dx), BF16), vmem((nx, tokens, dx), BF16), vmem((tokens, dx), F32),
        dma(4), dma(nx), dma(nx), dma(nx),
        dma(ny, nx * zper), dma(ny, nx * zper), dma(ny), dma(ny),
        dma(2, rows), dma(2, rows), dma(2, nz), dma(2, nz), dma(2, rows), dma(2, rows),
        dma(rows), dma(rows), dma(nz), dma(nz), dma(1), dma(1),
        dma(nx), dma(nx),
    ]
    grad = jax.ShapeDtypeStruct((tokens, width), BF16)
    out, qg, kg, vg, wg = pl.pallas_call(
        functools.partial(kernel, nz, ny, nx),
        out_shape=(
            jax.ShapeDtypeStruct((tokens, dx), BF16), grad, grad, grad,
            jax.ShapeDtypeStruct((width, 64), F32),
        ),
        in_specs=[pl.BlockSpec(memory_space=pl.ANY)] * 5,
        out_specs=[pl.BlockSpec(memory_space=pltpu.VMEM)] * 5,
        scratch_shapes=scratch,
        compiler_params=pltpu.CompilerParams(
            collective_id=0, has_side_effects=True, vmem_limit_bytes=48 << 20,
        ),
    )(flat(queries), flat(keys), flat(values), out_weight, flat(upstream))
    pairs = lambda a: a.reshape(pair, length, a.shape[1])
    return pairs(out), pairs(qg), pairs(kg), pairs(vg), wg


def solution(mesh):
    return jax.shard_map(
        on_device,
        mesh=mesh,
        in_specs=(
            P(None, "seq", "head"),
            P(None, "seq", "head"),
            P(None, "seq", "head"),
            P("head", None),
            P(None, "seq", "head"),
        ),
        out_specs=(
            P(None, "seq", "head"),
            P(None, "seq", "head"),
            P(None, "seq", "head"),
            P(None, "seq", "head"),
            P("head", "seq"),
        ),
        check_vma=False,
    )
```

```python
import functools

import jax
import jax.numpy as jnp
from jax import lax
from jax.experimental import pallas as pl
from jax.experimental.pallas import tpu as pltpu
from jax.sharding import PartitionSpec as P

MESH = pl.DeviceIdType.MESH
SPAN = 64
HEAD_DIM = 128
EPS = 1e-06
NZ = 8
NY = 4
F32 = jnp.float32
BF16 = jnp.bfloat16


def nn(a, b):
    return lax.dot_general(a, b, (((1,), (0,)), ((), ())), preferred_element_type=F32)


def nt(a, b):
    return lax.dot_general(a, b, (((1,), (1,)), ((), ())), preferred_element_type=F32)


def tn(a, b):
    return lax.dot_general(a, b, (((0,), (0,)), ((), ())), preferred_element_type=F32)


def kernel(
    nz, ny, nx,
    q_hbm, k_hbm, v_hbm, w_hbm, up_hbm,
    out_ref, qg_ref, kg_ref, vg_ref, wg_ref,
    q, k, v, w, upf, upt, upr,
    ssend, srow, zsend, zbuf, tsend, trow,
    wts, att, normed, scale, hidden, hg, ag, kacc, vacc,
    hsend, hrow, wsend, wrow, osend, orecv, oown,
    in_sem, w_sem, ups_sem, upr_sem, rls_sem, rlr_sem, ys_sem, yr_sem,
    xgs_sem, xgr_sem, xrs_sem, xrr_sem, pfs_sem, pfr_sem,
    s1s, s1r, s2s, s2r, s3s, s3r, hs_sem, hr_sem, ws_sem, wr_sem, os_sem, or_sem,
):
    rows = 2 * ny
    heads = q.shape[1] // HEAD_DIM
    width = q.shape[1]
    tokens = q.shape[0]
    dx = up_hbm.shape[1]
    sl = width // rows
    pieces = HEAD_DIM // sl
    zper = dx // (ny * 128)
    half = width // 2

    s_me = lax.axis_index("seq")
    x_me = lax.axis_index("head")
    z_me = s_me // rows
    r_me = s_me % rows
    y_me = r_me // 2
    c_me = r_me % 2
    x_up = (x_me + 1) % nx
    x_down = (x_me + nx - 1) % nx
    x_far = (x_me + 2) % nx
    partner = (z_me * rows + y_me * 2 + 1 - c_me, x_me)

    def at_row(r):
        return (z_me * rows + r, x_me)

    def at_z(z):
        return (z * rows + r_me, x_me)

    def at_x(x):
        return (s_me, x)

    waits = []

    def send(src, dst, ssem, rsem, device):
        copy = pltpu.make_async_remote_copy(
            src_ref=src, dst_ref=dst, send_sem=ssem, recv_sem=rsem,
            device_id=device, device_id_type=MESH,
        )
        copy.start()
        waits.append(copy)
        return copy

    loads = [
        pltpu.make_async_copy(src, dst, in_sem.at[i])
        for i, (src, dst) in enumerate(
            ((k_hbm, k), (v_hbm, v), (q_hbm, q), (up_hbm, upf.at[x_me]))
        )
    ]
    w_loads = [
        pltpu.make_async_copy(w_hbm.at[:, pl.ds(j * dx, dx)], w.at[j], w_sem.at[j])
        for j in range(nx)
    ]
    for copy in loads + w_loads:
        copy.start()

    barrier = pltpu.get_barrier_semaphore()
    for j in range(1, nz):
        pl.semaphore_signal(barrier, inc=1, device_id=at_z((z_me + j) % nz), device_id_type=MESH)
    for j in range(1, rows):
        pl.semaphore_signal(barrier, inc=1, device_id=at_row((r_me + j) % rows), device_id_type=MESH)
    for j in range(1, nx):
        pl.semaphore_signal(barrier, inc=1, device_id=at_x((x_me + j) % nx), device_id_type=MESH)

    def lanes(h):
        return slice(h * HEAD_DIM, (h + 1) * HEAD_DIM)

    def span(p):
        return slice(p * SPAN, (p + 1) * SPAN)

    def exchange_slices(which, src, into, ssem, rsem):
        copies = []
        for j in range(1, rows):
            peer = (r_me + j) % rows
            copies.append(send(
                src.at[which, peer], into.at[which, r_me],
                ssem.at[which, j], rsem.at[which, j], at_row(peer),
            ))
        into[which, r_me] = src[which, r_me]
        return copies

    def put_terms(which, p, h, term):
        term = term.astype(BF16)
        for i in range(pieces):
            ssend[which, h * pieces + i, p] = term[i * sl:(i + 1) * sl]

    def row_sums(which, first, copies):
        for copy in copies:
            copy.wait_recv()
        low = srow[which, 0, first].astype(F32)
        high = srow[which, 0, 1 - first].astype(F32)
        for r in range(1, rows):
            low = low + srow[which, r, first].astype(F32)
            high = high + srow[which, r, 1 - first].astype(F32)
        zsend[which, 0] = low.astype(BF16)
        zsend[which, 1] = (low + high).astype(BF16)
        zbuf[which, z_me] = low.astype(BF16)
        return [
            send(
                zsend.at[which, (z_me + j) // nz], zbuf.at[which, z_me],
                s2s.at[which, j], s2r.at[which, j], at_z((z_me + j) % nz),
            )
            for j in range(1, nz)
        ]

    def prefixes(which, first, copies):
        for copy in copies:
            copy.wait_recv()
        below = jnp.zeros((sl, HEAD_DIM), F32)
        total = jnp.zeros((sl, HEAD_DIM), F32)
        for j in range(nz):
            term = zbuf[which, j].astype(F32)
            total = total + term
            below = below + jnp.where(j < z_me, term, 0.0)
        for r in range(rows):
            tsend[which, r, first] = below.astype(BF16)
            below = below + srow[which, r, first].astype(F32)
        for r in range(rows - 1, -1, -1):
            tsend[which, r, 1 - first] = total.astype(BF16)
            total = total + srow[which, r, 1 - first].astype(F32)
        return exchange_slices(which, tsend, trow, s3s, s3r)

    def state_of(which, p, h):
        return jnp.concatenate(
            [trow[which, h * pieces + i, p] for i in range(pieces)], axis=0
        )

    loads[0].wait()
    loads[1].wait()
    for h in range(heads):
        for p in range(2):
            put_terms(0, p, h, tn(k[span(p), lanes(h)], v[span(p), lanes(h)]))
    pl.semaphore_wait(barrier, rows + nz + nx - 3)

    step1 = exchange_slices(0, ssend, srow, s1s, s1r)
    from_down = send(up_hbm, upf.at[x_me], ups_sem.at[0], upr_sem.at[0], at_x(x_up))
    from_up = send(up_hbm, upf.at[x_me], ups_sem.at[1], upr_sem.at[1], at_x(x_down))

    loads[3].wait()
    for b in range(zper):
        for yy in range(ny):
            at = (b * ny + yy) * 128
            upt[yy, b] = jnp.transpose(upf[x_me, :, at:at + 128].astype(F32)).astype(BF16)
    over_y = []
    for m in range(1, ny):
        peer = (y_me + m) % ny
        over_y.append(send(
            upt.at[peer], upr.at[c_me, x_me, y_me], ys_sem.at[m], yr_sem.at[m],
            at_row(peer * 2 + c_me),
        ))
    upr[c_me, x_me, y_me] = upt[y_me]

    loads[2].wait()
    row_i = lax.broadcasted_iota(jnp.int32, (2 * SPAN, 2 * SPAN), 0)
    col_i = lax.broadcasted_iota(jnp.int32, (2 * SPAN, 2 * SPAN), 1)
    mask = (row_i >= col_i) & ((row_i < SPAN) | (col_i >= SPAN))
    for h in range(heads):
        weights = jnp.where(mask, nt(q[:, lanes(h)], k[:, lanes(h)]), 0.0).astype(BF16)
        wts[h] = weights
        att[:, lanes(h)] = nn(weights, v[:, lanes(h)])

    step2 = row_sums(0, 0, step1)

    for copy in w_loads:
        copy.wait()
    hg[...] = nt(upf[x_me], w[x_me])
    for copy in over_y:
        copy.wait_recv()
    from_down.wait_recv()
    low_half = send(
        upf.at[x_down, pl.ds(0, tokens // 2)], upf.at[x_down, pl.ds(0, tokens // 2)],
        rls_sem.at[0], rlr_sem.at[0], at_x(x_up),
    )
    from_up.wait_recv()
    high_half = send(
        upf.at[x_up, pl.ds(tokens // 2, tokens // 2)], upf.at[x_up, pl.ds(tokens // 2, tokens // 2)],
        rls_sem.at[1], rlr_sem.at[1], at_x(x_down),
    )
    cols_down = send(upr.at[c_me, x_me], upr.at[c_me, x_me], xgs_sem.at[0], xgr_sem.at[0], at_x(x_up))
    cols_up = send(upr.at[c_me, x_me], upr.at[c_me, x_me], xgs_sem.at[1], xgr_sem.at[1], at_x(x_down))
    to_partner = [send(upr.at[c_me, x_me], upr.at[c_me, x_me], pfs_sem.at[0], pfr_sem.at[0], partner)]
    hg[...] = hg[...] + nt(upf[x_down], w[x_down])
    hg[...] = hg[...] + nt(upf[x_up], w[x_up])

    step3 = prefixes(0, 0, step2)

    low_half.wait_recv()
    high_half.wait_recv()
    hg[...] = hg[...] + nt(upf[x_far], w[x_far])
    cols_down.wait_recv()
    hy = ny // 2
    low_cols = send(
        upr.at[c_me, x_down, pl.ds(0, hy)], upr.at[c_me, x_down, pl.ds(0, hy)],
        xrs_sem.at[0], xrr_sem.at[0], at_x(x_up),
    )
    cols_up.wait_recv()
    high_cols = send(
        upr.at[c_me, x_up, pl.ds(hy, hy)], upr.at[c_me, x_up, pl.ds(hy, hy)],
        xrs_sem.at[1], xrr_sem.at[1], at_x(x_down),
    )
    for i, slot in enumerate((x_down, x_up)):
        to_partner.append(send(
            upr.at[c_me, slot], upr.at[c_me, slot], pfs_sem.at[1 + i], pfr_sem.at[1 + i], partner,
        ))

    for copy in step3:
        copy.wait_recv()
    for h in range(heads):
        local = att[:, lanes(h)] + jnp.concatenate(
            [nn(q[span(p), lanes(h)], state_of(0, p, h)) for p in range(2)], axis=0
        )
        deviation = jnp.sqrt(jnp.mean(local * local, axis=-1, keepdims=True) + EPS)
        unit = local / deviation
        normed[:, lanes(h)] = unit
        scale[:, lanes(h)] = jnp.broadcast_to(deviation, (2 * SPAN, HEAD_DIM))
        hidden[:, lanes(h)] = unit.astype(BF16)
        hsend[lanes(h), :] = jnp.transpose(unit).astype(BF16)

    over_row = []
    for j in range(1, rows):
        peer = (r_me + j) % rows
        over_row.append(send(
            hsend.at[pl.ds(pl.multiple_of((peer % 2) * half, 128), half)], hrow.at[r_me],
            hs_sem.at[j], hr_sem.at[j], at_row(peer),
        ))
    hrow[r_me] = hsend[pl.ds(pl.multiple_of(c_me * half, 128), half)]

    for h in range(heads):
        unit = normed[:, lanes(h)]
        grad = hg[:, lanes(h)]
        inner = jnp.mean(grad * unit, axis=-1, keepdims=True)
        attn = ((grad - unit * inner) / scale[:, lanes(h)]).astype(BF16)
        ag[:, lanes(h)] = attn
        for p in range(2):
            put_terms(1, p, h, tn(q[span(p), lanes(h)], attn[span(p)]))
    back1 = exchange_slices(1, ssend, srow, s1s, s1r)

    over_x = []
    for j in range(1, nx):
        peer = (x_me + j) % nx
        osend[j] = nn(hidden[...], w[peer]).astype(BF16)
        over_x.append(send(osend.at[j], orecv.at[j], os_sem.at[j], or_sem.at[j], at_x(peer)))

    low_cols.wait_recv()
    high_cols.wait_recv()
    to_partner.append(send(
        upr.at[c_me, x_far], upr.at[c_me, x_far], pfs_sem.at[3], pfr_sem.at[3], partner,
    ))

    back2 = row_sums(1, 1, back1)

    for copy in over_row + to_partner:
        copy.wait_recv()
    feats = jnp.concatenate([hrow[r] for r in range(rows)], axis=1)
    for xx in range(nx):
        cols = jnp.concatenate(
            [
                jnp.concatenate([upr[r % 2, xx, r // 2, b] for r in range(rows)], axis=1)
                for b in range(zper)
            ],
            axis=0,
        )
        part = nt(cols, feats).astype(BF16)
        for b in range(zper):
            for c in range(2):
                at = b * 128 + c * 64
                wsend[xx * zper + b, c] = part[at:at + 64]
    for j in range(1, nz):
        peer = (z_me + j) % nz
        for c in range(2):
            send(
                wsend.at[peer, c], wrow.at[z_me, c_me], ws_sem.at[j, c], wr_sem.at[j, c_me],
                (peer * rows + y_me * 2 + c, x_me),
            )
    over_z = [send(
        wsend.at[z_me, 1 - c_me], wrow.at[z_me, c_me], ws_sem.at[0, 0], wr_sem.at[0, 0], partner,
    )]
    for j in range(1, nz):
        for c in range(2):
            over_z.append(pltpu.make_async_remote_copy(
                src_ref=wsend.at[z_me, c], dst_ref=wrow.at[z_me, c],
                send_sem=ws_sem.at[j, c], recv_sem=wr_sem.at[j, c],
                device_id=partner, device_id_type=MESH,
            ))
    wrow[z_me, c_me] = wsend[z_me, c_me]

    oown[...] = nn(hidden[...], w[x_me])
    for h in range(heads):
        attn = ag[:, lanes(h)]
        diffs = jnp.where(mask, nt(attn, v[:, lanes(h)]), 0.0).astype(BF16)
        qg_ref[:, lanes(h)] = (
            nn(diffs, k[:, lanes(h)])
            + jnp.concatenate([nt(attn[span(p)], state_of(0, p, h)) for p in range(2)], axis=0)
        ).astype(BF16)
        kacc[:, lanes(h)] = tn(diffs, q[:, lanes(h)])
        vacc[:, lanes(h)] = tn(wts[h], attn)

    back3 = prefixes(1, 1, back2)

    total = oown[...]
    for j, copy in enumerate(over_x):
        copy.wait_recv()
        total = total + orecv[j + 1].astype(F32)
    out_ref[...] = total.astype(BF16)

    for copy in back3:
        copy.wait_recv()
    for h in range(heads):
        later = [state_of(1, p, h) for p in range(2)]
        kg_ref[:, lanes(h)] = (
            kacc[:, lanes(h)]
            + jnp.concatenate([nt(v[span(p), lanes(h)], later[p]) for p in range(2)], axis=0)
        ).astype(BF16)
        vg_ref[:, lanes(h)] = (
            vacc[:, lanes(h)]
            + jnp.concatenate([nn(k[span(p), lanes(h)], later[p]) for p in range(2)], axis=0)
        ).astype(BF16)

    for copy in over_z:
        copy.wait_recv()
    for c in range(2):
        total = wrow[0, c].astype(F32)
        for j in range(1, nz):
            total = total + wrow[j, c].astype(F32)
        wg_ref[:, c * half:(c + 1) * half] = total
    for copy in waits:
        copy.wait_send()


def write_out(*refs):
    count = len(refs) // 2
    sem = refs[-1]
    copies = [
        pltpu.make_async_copy(refs[i], refs[count + i], sem.at[i]) for i in range(count)
    ]
    for copy in copies:
        copy.start()
    for copy in copies:
        copy.wait()


def on_device(queries, keys, values, out_weight, upstream):
    nx = lax.axis_size("head")
    nz, ny = NZ, NY
    rows = 2 * ny
    pair, length, width = queries.shape
    tokens = pair * length
    heads = width // HEAD_DIM
    dx = upstream.shape[2]
    sl = width // rows
    half = width // 2
    zper = dx // (ny * 128)
    flat = lambda a: a.reshape(tokens, a.shape[2])
    vmem = pltpu.VMEM
    dma = lambda *shape: pltpu.SemaphoreType.DMA(shape)
    state = vmem((2, rows, 2, sl, HEAD_DIM), BF16)
    narrow = vmem((tokens, width), BF16)
    wide = vmem((tokens, width), F32)
    scratch = [
        narrow, narrow, narrow,
        vmem((nx, width, dx), BF16),
        vmem((nx, tokens, dx), BF16),
        vmem((ny, zper, 128, tokens), BF16),
        vmem((2, nx, ny, zper, 128, tokens), BF16),
        state, state,
        vmem((2, 2, sl, HEAD_DIM), BF16),
        vmem((2, nz, sl, HEAD_DIM), BF16),
        state, state,
        vmem((heads, tokens, tokens), BF16),
        wide, wide, wide, narrow, wide, narrow, wide, wide,
        vmem((width, tokens), BF16), vmem((rows, half, tokens), BF16),
        vmem((nz, 2, 64, half), BF16), vmem((nz, 2, 64, half), BF16),
        vmem((nx, tokens, dx), BF16), vmem((nx, tokens, dx), BF16), vmem((tokens, dx), F32),
        dma(4), dma(nx), dma(2), dma(2), dma(2), dma(2), dma(ny), dma(ny),
        dma(2), dma(2), dma(2), dma(2), dma(4), dma(4),
        dma(2, rows), dma(2, rows), dma(2, nz), dma(2, nz), dma(2, rows), dma(2, rows),
        dma(rows), dma(rows), dma(nz, 2), dma(nz, 2), dma(nx), dma(nx),
    ]
    grad = jax.ShapeDtypeStruct((tokens, width), BF16)
    shapes = (
        jax.ShapeDtypeStruct((tokens, dx), BF16), grad, grad, grad,
        jax.ShapeDtypeStruct((64, width), F32),
    )
    results = pl.pallas_call(
        functools.partial(kernel, nz, ny, nx),
        out_shape=shapes,
        in_specs=[pl.BlockSpec(memory_space=pltpu.HBM)] * 5,
        out_specs=[pl.BlockSpec(memory_space=pltpu.VMEM)] * 5,
        scratch_shapes=scratch,
        compiler_params=pltpu.CompilerParams(
            collective_id=0, has_side_effects=True, vmem_limit_bytes=48 << 20,
        ),
    )(*[pltpu.with_memory_space_constraint(a, pltpu.HBM) for a in (flat(queries), flat(keys), flat(values), out_weight, flat(upstream))])
    out, qg, kg, vg, wg = pl.pallas_call(
        write_out,
        out_shape=shapes,
        in_specs=[pl.BlockSpec(memory_space=pl.ANY)] * 5,
        out_specs=[pl.BlockSpec(memory_space=pltpu.HBM)] * 5,
        scratch_shapes=[dma(5)],
        compiler_params=pltpu.CompilerParams(vmem_limit_bytes=4 << 20),
    )(*results)
    pairs = lambda a: a.reshape(pair, length, a.shape[1])
    return pairs(out), pairs(qg), pairs(kg), pairs(vg), wg.T


def solution(mesh):
    return jax.shard_map(
        on_device,
        mesh=mesh,
        in_specs=(
            P(None, "seq", "head"),
            P(None, "seq", "head"),
            P(None, "seq", "head"),
            P("head", None),
            P(None, "seq", "head"),
        ),
        out_specs=(
            P(None, "seq", "head"),
            P(None, "seq", "head"),
            P(None, "seq", "head"),
            P(None, "seq", "head"),
            P("head", "seq"),
        ),
        check_vma=False,
    )
```

```python
import functools

import jax
import jax.numpy as jnp
from jax import lax
from jax.experimental import pallas as pl
from jax.experimental.pallas import tpu as pltpu
from jax.sharding import PartitionSpec as P

MESH = pl.DeviceIdType.MESH
SPAN = 64
HEAD_DIM = 128
EPS = 1e-06
NZ = 8
NY = 4
F32 = jnp.float32
BF16 = jnp.bfloat16


def nn(a, b):
    return lax.dot_general(a, b, (((1,), (0,)), ((), ())), preferred_element_type=F32)


def nt(a, b):
    return lax.dot_general(a, b, (((1,), (1,)), ((), ())), preferred_element_type=F32)


def tn(a, b):
    return lax.dot_general(a, b, (((0,), (0,)), ((), ())), preferred_element_type=F32)


def kernel(
    nz, ny, nx,
    q_hbm, k_hbm, v_hbm, w_hbm, up_hbm,
    out_ref, qg_ref, kg_ref, vg_ref, wg_ref,
    q, k, v, w, upf, upt, upr,
    ssend, srow, zsend, zbuf, tsend, trow,
    wts, att, normed, scale, hidden, hg, ag, kacc, vacc,
    hsend, hrow, wsend, wrow, wrel, wfar, wout, osend, orel, orecv, oown,
    in_sem, w_sem, ups_sem, upr_sem, rls_sem, rlr_sem, ys_sem, yr_sem,
    xgs_sem, xgr_sem, xrs_sem, xrr_sem, pfs_sem, pfr_sem,
    s1s, s1r, s2s, s2r, s3s, s3r, hs_sem, hr_sem, ws_sem, wr_sem, os_sem, or_sem,
):
    rows = 2 * ny
    heads = q.shape[1] // HEAD_DIM
    width = q.shape[1]
    tokens = q.shape[0]
    dx = up_hbm.shape[1]
    sl = width // rows
    pieces = HEAD_DIM // sl
    zper = dx // (ny * 128)
    half = width // 2

    s_me = lax.axis_index("seq")
    x_me = lax.axis_index("head")
    z_me = s_me // rows
    r_me = s_me % rows
    y_me = r_me // 2
    c_me = r_me % 2
    x_up = (x_me + 1) % nx
    x_down = (x_me + nx - 1) % nx
    x_far = (x_me + 2) % nx
    partner = (z_me * rows + y_me * 2 + 1 - c_me, x_me)

    def at_row(r):
        return (z_me * rows + r, x_me)

    def at_z(z):
        return (z * rows + r_me, x_me)

    def at_x(x):
        return (s_me, x)

    waits = []

    def send(src, dst, ssem, rsem, device):
        copy = pltpu.make_async_remote_copy(
            src_ref=src, dst_ref=dst, send_sem=ssem, recv_sem=rsem,
            device_id=device, device_id_type=MESH,
        )
        copy.start()
        waits.append(copy)
        return copy

    loads = [
        pltpu.make_async_copy(src, dst, in_sem.at[i])
        for i, (src, dst) in enumerate(
            ((k_hbm, k), (v_hbm, v), (q_hbm, q), (up_hbm, upf.at[x_me]))
        )
    ]
    w_loads = [
        pltpu.make_async_copy(w_hbm.at[:, pl.ds(j * dx, dx)], w.at[j], w_sem.at[j])
        for j in range(nx)
    ]
    for copy in loads + w_loads:
        copy.start()

    barrier = pltpu.get_barrier_semaphore()
    for j in range(1, nz):
        pl.semaphore_signal(barrier, inc=1, device_id=at_z((z_me + j) % nz), device_id_type=MESH)
    for j in range(1, rows):
        pl.semaphore_signal(barrier, inc=1, device_id=at_row((r_me + j) % rows), device_id_type=MESH)
    for j in range(1, nx):
        pl.semaphore_signal(barrier, inc=1, device_id=at_x((x_me + j) % nx), device_id_type=MESH)

    def lanes(h):
        return slice(h * HEAD_DIM, (h + 1) * HEAD_DIM)

    def span(p):
        return slice(p * SPAN, (p + 1) * SPAN)

    def exchange_slices(which, src, into, ssem, rsem):
        copies = []
        for j in range(1, rows):
            peer = (r_me + j) % rows
            copies.append(send(
                src.at[which, peer], into.at[which, r_me],
                ssem.at[which, j], rsem.at[which, j], at_row(peer),
            ))
        into[which, r_me] = src[which, r_me]
        return copies

    def put_terms(which, p, h, term):
        term = term.astype(BF16)
        for i in range(pieces):
            ssend[which, h * pieces + i, p] = term[i * sl:(i + 1) * sl]

    def row_sums(which, first, copies):
        for copy in copies:
            copy.wait_recv()
        low = srow[which, 0, first].astype(F32)
        high = srow[which, 0, 1 - first].astype(F32)
        for r in range(1, rows):
            low = low + srow[which, r, first].astype(F32)
            high = high + srow[which, r, 1 - first].astype(F32)
        zsend[which, 0] = low.astype(BF16)
        zsend[which, 1] = (low + high).astype(BF16)
        zbuf[which, z_me] = low.astype(BF16)
        return [
            send(
                zsend.at[which, (z_me + j) // nz], zbuf.at[which, z_me],
                s2s.at[which, j], s2r.at[which, j], at_z((z_me + j) % nz),
            )
            for j in range(1, nz)
        ]

    def prefixes(which, first, copies):
        for copy in copies:
            copy.wait_recv()
        below = jnp.zeros((sl, HEAD_DIM), F32)
        total = jnp.zeros((sl, HEAD_DIM), F32)
        for j in range(nz):
            term = zbuf[which, j].astype(F32)
            total = total + term
            below = below + jnp.where(j < z_me, term, 0.0)
        for r in range(rows):
            tsend[which, r, first] = below.astype(BF16)
            below = below + srow[which, r, first].astype(F32)
        for r in range(rows - 1, -1, -1):
            tsend[which, r, 1 - first] = total.astype(BF16)
            total = total + srow[which, r, 1 - first].astype(F32)
        return exchange_slices(which, tsend, trow, s3s, s3r)

    def state_of(which, p, h):
        return jnp.concatenate(
            [trow[which, h * pieces + i, p] for i in range(pieces)], axis=0
        )

    loads[0].wait()
    loads[1].wait()
    for h in range(heads):
        for p in range(2):
            put_terms(0, p, h, tn(k[span(p), lanes(h)], v[span(p), lanes(h)]))
    pl.semaphore_wait(barrier, rows + nz + nx - 3)

    step1 = exchange_slices(0, ssend, srow, s1s, s1r)
    from_down = send(up_hbm, upf.at[x_me], ups_sem.at[0], upr_sem.at[0], at_x(x_up))
    from_up = send(up_hbm, upf.at[x_me], ups_sem.at[1], upr_sem.at[1], at_x(x_down))

    loads[3].wait()
    for b in range(zper):
        for yy in range(ny):
            at = (b * ny + yy) * 128
            upt[yy, b] = jnp.transpose(upf[x_me, :, at:at + 128].astype(F32)).astype(BF16)
    over_y = []
    for m in range(1, ny):
        peer = (y_me + m) % ny
        over_y.append(send(
            upt.at[peer], upr.at[c_me, x_me, y_me], ys_sem.at[m], yr_sem.at[m],
            at_row(peer * 2 + c_me),
        ))
    upr[c_me, x_me, y_me] = upt[y_me]

    loads[2].wait()
    row_i = lax.broadcasted_iota(jnp.int32, (2 * SPAN, 2 * SPAN), 0)
    col_i = lax.broadcasted_iota(jnp.int32, (2 * SPAN, 2 * SPAN), 1)
    mask = (row_i >= col_i) & ((row_i < SPAN) | (col_i >= SPAN))
    for h in range(heads):
        weights = jnp.where(mask, nt(q[:, lanes(h)], k[:, lanes(h)]), 0.0).astype(BF16)
        wts[h] = weights
        att[:, lanes(h)] = nn(weights, v[:, lanes(h)])

    step2 = row_sums(0, 0, step1)

    for copy in w_loads:
        copy.wait()
    hg[...] = nt(upf[x_me], w[x_me])
    for copy in over_y:
        copy.wait_recv()
    from_down.wait_recv()
    low_half = send(
        upf.at[x_down, pl.ds(0, tokens // 2)], upf.at[x_down, pl.ds(0, tokens // 2)],
        rls_sem.at[0], rlr_sem.at[0], at_x(x_up),
    )
    from_up.wait_recv()
    high_half = send(
        upf.at[x_up, pl.ds(tokens // 2, tokens // 2)], upf.at[x_up, pl.ds(tokens // 2, tokens // 2)],
        rls_sem.at[1], rlr_sem.at[1], at_x(x_down),
    )
    cols_down = send(upr.at[c_me, x_me], upr.at[c_me, x_me], xgs_sem.at[0], xgr_sem.at[0], at_x(x_up))
    cols_up = send(upr.at[c_me, x_me], upr.at[c_me, x_me], xgs_sem.at[1], xgr_sem.at[1], at_x(x_down))
    to_partner = [send(upr.at[c_me, x_me], upr.at[c_me, x_me], pfs_sem.at[0], pfr_sem.at[0], partner)]
    hg[...] = hg[...] + nt(upf[x_down], w[x_down])
    hg[...] = hg[...] + nt(upf[x_up], w[x_up])

    step3 = prefixes(0, 0, step2)

    low_half.wait_recv()
    high_half.wait_recv()
    hg[...] = hg[...] + nt(upf[x_far], w[x_far])
    cols_down.wait_recv()
    hy = ny // 2
    low_cols = send(
        upr.at[c_me, x_down, pl.ds(0, hy)], upr.at[c_me, x_down, pl.ds(0, hy)],
        xrs_sem.at[0], xrr_sem.at[0], at_x(x_up),
    )
    cols_up.wait_recv()
    high_cols = send(
        upr.at[c_me, x_up, pl.ds(hy, hy)], upr.at[c_me, x_up, pl.ds(hy, hy)],
        xrs_sem.at[1], xrr_sem.at[1], at_x(x_down),
    )
    for i, slot in enumerate((x_down, x_up)):
        to_partner.append(send(
            upr.at[c_me, slot], upr.at[c_me, slot], pfs_sem.at[1 + i], pfr_sem.at[1 + i], partner,
        ))

    for copy in step3:
        copy.wait_recv()
    for h in range(heads):
        local = att[:, lanes(h)] + jnp.concatenate(
            [nn(q[span(p), lanes(h)], state_of(0, p, h)) for p in range(2)], axis=0
        )
        deviation = jnp.sqrt(jnp.mean(local * local, axis=-1, keepdims=True) + EPS)
        unit = local / deviation
        normed[:, lanes(h)] = unit
        scale[:, lanes(h)] = jnp.broadcast_to(deviation, (2 * SPAN, HEAD_DIM))
        hidden[:, lanes(h)] = unit.astype(BF16)
        hsend[lanes(h), :] = jnp.transpose(unit).astype(BF16)

    y_up = (y_me + 1) % ny
    y_down = (y_me + ny - 1) % ny
    for c in range(2):
        part = hsend.at[pl.ds(c * half, half)]
        send(part, hrow.at[r_me], hs_sem.at[0, c], hr_sem.at[0, c_me], at_row(y_up * 2 + c))
        send(part, hrow.at[r_me], hs_sem.at[1, c], hr_sem.at[1, c_me], at_row(y_down * 2 + c))
    from_partner = send(
        hsend.at[pl.ds(pl.multiple_of((1 - c_me) * half, 128), half)], hrow.at[r_me],
        hs_sem.at[3, 0], hr_sem.at[3, 0], partner,
    )
    hrow[r_me] = hsend[pl.ds(pl.multiple_of(c_me * half, 128), half)]

    for h in range(heads):
        unit = normed[:, lanes(h)]
        grad = hg[:, lanes(h)]
        inner = jnp.mean(grad * unit, axis=-1, keepdims=True)
        attn = ((grad - unit * inner) / scale[:, lanes(h)]).astype(BF16)
        ag[:, lanes(h)] = attn
        for p in range(2):
            put_terms(1, p, h, tn(q[span(p), lanes(h)], attn[span(p)]))
    back1 = exchange_slices(1, ssend, srow, s1s, s1r)

    mid = tokens // 2
    osend[0] = nn(hidden[...], w[x_far]).astype(BF16)
    out_low = send(osend.at[0, pl.ds(0, mid)], orel.at[0], os_sem.at[0], or_sem.at[0], at_x(x_up))
    out_high = send(osend.at[0, pl.ds(mid, mid)], orel.at[1], os_sem.at[1], or_sem.at[1], at_x(x_down))
    osend[1] = nn(hidden[...], w[x_up]).astype(BF16)
    over_x = [send(
        osend.at[1, pl.ds(mid, mid)], orecv.at[0, pl.ds(mid, mid)],
        os_sem.at[2], or_sem.at[2], at_x(x_up),
    )]
    osend[2] = nn(hidden[...], w[x_down]).astype(BF16)
    over_x.append(send(
        osend.at[2, pl.ds(0, mid)], orecv.at[1, pl.ds(0, mid)],
        os_sem.at[3], or_sem.at[3], at_x(x_down),
    ))

    low_cols.wait_recv()
    high_cols.wait_recv()
    to_partner.append(send(
        upr.at[c_me, x_far], upr.at[c_me, x_far], pfs_sem.at[3], pfr_sem.at[3], partner,
    ))

    oown[...] = nn(hidden[...], w[x_me])
    for h in range(heads):
        attn = ag[:, lanes(h)]
        diffs = jnp.where(mask, nt(attn, v[:, lanes(h)]), 0.0).astype(BF16)
        qg_ref[:, lanes(h)] = (
            nn(diffs, k[:, lanes(h)])
            + jnp.concatenate([nt(attn[span(p)], state_of(0, p, h)) for p in range(2)], axis=0)
        ).astype(BF16)
        kacc[:, lanes(h)] = tn(diffs, q[:, lanes(h)])
        vacc[:, lanes(h)] = tn(wts[h], attn)

    def arrived(into, sem):
        pltpu.make_async_remote_copy(
            src_ref=into, dst_ref=into, send_sem=hs_sem.at[3, 0], recv_sem=sem,
            device_id=partner, device_id_type=MESH,
        ).wait_recv()

    for c in range(2):
        arrived(hrow.at[y_down * 2 + c], hr_sem.at[0, c])
        arrived(hrow.at[y_up * 2 + c], hr_sem.at[1, c])
    slot = y_down * 2
    far_row = [send(hrow.at[slot], hrow.at[slot], hs_sem.at[2, 0], hr_sem.at[2, 0], at_row(y_up * 2 + c_me))]
    slot = y_up * 2 + 1
    far_row.append(
        send(hrow.at[slot], hrow.at[slot], hs_sem.at[2, 1], hr_sem.at[2, 1], at_row(y_down * 2 + c_me))
    )

    back2 = row_sums(1, 1, back1)

    out_low.wait_recv()
    osend[1, :mid] = (osend[1, :mid].astype(F32) + orel[0].astype(F32)).astype(BF16)
    over_x.append(send(
        osend.at[1, pl.ds(0, mid)], orecv.at[0, pl.ds(0, mid)],
        os_sem.at[4], or_sem.at[4], at_x(x_up),
    ))
    out_high.wait_recv()
    osend[2, mid:] = (osend[2, mid:].astype(F32) + orel[1].astype(F32)).astype(BF16)
    over_x.append(send(
        osend.at[2, pl.ds(mid, mid)], orecv.at[1, pl.ds(mid, mid)],
        os_sem.at[5], or_sem.at[5], at_x(x_down),
    ))

    for copy in far_row + [from_partner] + to_partner:
        copy.wait_recv()
    feats = jnp.concatenate([hrow[r] for r in range(rows)], axis=1)
    for xx in range(nx):
        cols = jnp.concatenate(
            [
                jnp.concatenate([upr[r % 2, xx, r // 2, b] for r in range(rows)], axis=1)
                for b in range(zper)
            ],
            axis=0,
        )
        part = nt(cols, feats).astype(BF16)
        for b in range(zper):
            for c in range(2):
                at = b * 128 + c * 64
                wsend[xx * zper + b, c] = part[at:at + 64]
    def z_at(step):
        return (z_me + step + nz) % nz

    def owner(z, c):
        return (z * rows + y_me * 2 + c, x_me)

    rel_up = send(wsend.at[z_at(3)], wrel.at[0], ws_sem.at[0, 0], wr_sem.at[5, 0], at_z(z_at(1)))
    rel_down = send(wsend.at[z_at(-3)], wrel.at[1], ws_sem.at[0, 1], wr_sem.at[5, 1], at_z(z_at(-1)))
    far_up = send(wsend.at[z_at(4), 0], wfar.at[0], ws_sem.at[1, 0], wr_sem.at[6, 0], at_z(z_at(2)))
    far_down = send(wsend.at[z_at(4), 1], wfar.at[1], ws_sem.at[1, 1], wr_sem.at[6, 1], at_z(z_at(-2)))
    for i, step in enumerate((1, -1)):
        for c in range(2):
            send(
                wsend.at[z_at(step), c], wrow.at[i, c_me],
                ws_sem.at[2 + i, c], wr_sem.at[i, c_me], owner(z_at(step), c),
            )
    swap = send(wsend.at[z_me, 1 - c_me], wrow.at[4, c_me], ws_sem.at[4, 0], wr_sem.at[4, 0], partner)
    wrow[4, c_me] = wsend[z_me, c_me]

    back3 = prefixes(1, 1, back2)

    for copy in (rel_up, rel_down, far_up, far_down):
        copy.wait_recv()
    for i, step in enumerate((2, -2)):
        for c in range(2):
            term = wsend[z_at(step), c].astype(F32) + wrel[i, c].astype(F32)
            if c == i:
                term = term + wfar[i].astype(F32)
            wout[i, c] = term.astype(BF16)
            send(
                wout.at[i, c], wrow.at[2 + i, c_me],
                ws_sem.at[5 + i, c], wr_sem.at[2 + i, c_me], owner(z_at(step), c),
            )

    total = oown[...]
    for copy in over_x:
        copy.wait_recv()
    out_ref[...] = (total + orecv[0].astype(F32) + orecv[1].astype(F32)).astype(BF16)

    for copy in back3:
        copy.wait_recv()
    for h in range(heads):
        later = [state_of(1, p, h) for p in range(2)]
        kg_ref[:, lanes(h)] = (
            kacc[:, lanes(h)]
            + jnp.concatenate([nt(v[span(p), lanes(h)], later[p]) for p in range(2)], axis=0)
        ).astype(BF16)
        vg_ref[:, lanes(h)] = (
            vacc[:, lanes(h)]
            + jnp.concatenate([nn(k[span(p), lanes(h)], later[p]) for p in range(2)], axis=0)
        ).astype(BF16)

    swap.wait_recv()
    for i in range(4):
        for c in range(2):
            arrived(wrow.at[i, c], wr_sem.at[i, c])
    for c in range(2):
        total = wrow[0, c].astype(F32)
        for i in range(1, 5):
            total = total + wrow[i, c].astype(F32)
        wg_ref[:, c * half:(c + 1) * half] = total
    for copy in waits:
        copy.wait_send()


def write_out(*refs):
    count = len(refs) // 2
    sem = refs[-1]
    copies = [
        pltpu.make_async_copy(refs[i], refs[count + i], sem.at[i]) for i in range(count)
    ]
    for copy in copies:
        copy.start()
    for copy in copies:
        copy.wait()


def on_device(queries, keys, values, out_weight, upstream):
    nx = lax.axis_size("head")
    nz, ny = NZ, NY
    rows = 2 * ny
    pair, length, width = queries.shape
    tokens = pair * length
    heads = width // HEAD_DIM
    dx = upstream.shape[2]
    sl = width // rows
    half = width // 2
    zper = dx // (ny * 128)
    flat = lambda a: a.reshape(tokens, a.shape[2])
    vmem = pltpu.VMEM
    dma = lambda *shape: pltpu.SemaphoreType.DMA(shape)
    state = vmem((2, rows, 2, sl, HEAD_DIM), BF16)
    narrow = vmem((tokens, width), BF16)
    wide = vmem((tokens, width), F32)
    scratch = [
        narrow, narrow, narrow,
        vmem((nx, width, dx), BF16),
        vmem((nx, tokens, dx), BF16),
        vmem((ny, zper, 128, tokens), BF16),
        vmem((2, nx, ny, zper, 128, tokens), BF16),
        state, state,
        vmem((2, 2, sl, HEAD_DIM), BF16),
        vmem((2, nz, sl, HEAD_DIM), BF16),
        state, state,
        vmem((heads, tokens, tokens), BF16),
        wide, wide, wide, narrow, wide, narrow, wide, wide,
        vmem((width, tokens), BF16), vmem((rows, half, tokens), BF16),
        vmem((nz, 2, 64, half), BF16), vmem((5, 2, 64, half), BF16),
        vmem((2, 2, 64, half), BF16), vmem((2, 64, half), BF16), vmem((2, 2, 64, half), BF16),
        vmem((3, tokens, dx), BF16), vmem((2, tokens // 2, dx), BF16),
        vmem((2, tokens, dx), BF16), vmem((tokens, dx), F32),
        dma(4), dma(nx), dma(2), dma(2), dma(2), dma(2), dma(ny), dma(ny),
        dma(2), dma(2), dma(2), dma(2), dma(4), dma(4),
        dma(2, rows), dma(2, rows), dma(2, nz), dma(2, nz), dma(2, rows), dma(2, rows),
        dma(4, 2), dma(4, 2), dma(7, 2), dma(7, 2), dma(6), dma(6),
    ]
    grad = jax.ShapeDtypeStruct((tokens, width), BF16)
    shapes = (
        jax.ShapeDtypeStruct((tokens, dx), BF16), grad, grad, grad,
        jax.ShapeDtypeStruct((64, width), F32),
    )
    results = pl.pallas_call(
        functools.partial(kernel, nz, ny, nx),
        out_shape=shapes,
        in_specs=[pl.BlockSpec(memory_space=pltpu.HBM)] * 5,
        out_specs=[pl.BlockSpec(memory_space=pltpu.VMEM)] * 5,
        scratch_shapes=scratch,
        compiler_params=pltpu.CompilerParams(
            collective_id=0, has_side_effects=True, vmem_limit_bytes=48 << 20,
        ),
    )(*[pltpu.with_memory_space_constraint(a, pltpu.HBM) for a in (flat(queries), flat(keys), flat(values), out_weight, flat(upstream))])
    out, qg, kg, vg, wg = pl.pallas_call(
        write_out,
        out_shape=shapes,
        in_specs=[pl.BlockSpec(memory_space=pl.ANY)] * 5,
        out_specs=[pl.BlockSpec(memory_space=pltpu.HBM)] * 5,
        scratch_shapes=[dma(5)],
        compiler_params=pltpu.CompilerParams(vmem_limit_bytes=4 << 20),
    )(*results)
    pairs = lambda a: a.reshape(pair, length, a.shape[1])
    return pairs(out), pairs(qg), pairs(kg), pairs(vg), wg.T


def solution(mesh):
    return jax.shard_map(
        on_device,
        mesh=mesh,
        in_specs=(
            P(None, "seq", "head"),
            P(None, "seq", "head"),
            P(None, "seq", "head"),
            P("head", None),
            P(None, "seq", "head"),
        ),
        out_specs=(
            P(None, "seq", "head"),
            P(None, "seq", "head"),
            P(None, "seq", "head"),
            P(None, "seq", "head"),
            P("head", "seq"),
        ),
        check_vma=False,
    )
```

```python
import functools

import jax
import jax.numpy as jnp
from jax import lax
from jax.experimental import pallas as pl
from jax.experimental.pallas import tpu as pltpu
from jax.sharding import PartitionSpec as P

MESH = pl.DeviceIdType.MESH
SPAN = 64
HEAD_DIM = 128
EPS = 1e-06
NZ = 8
NY = 4
F32 = jnp.float32
BF16 = jnp.bfloat16


def nn(a, b):
    return lax.dot_general(a, b, (((1,), (0,)), ((), ())), preferred_element_type=F32)


def nt(a, b):
    return lax.dot_general(a, b, (((1,), (1,)), ((), ())), preferred_element_type=F32)


def tn(a, b):
    return lax.dot_general(a, b, (((0,), (0,)), ((), ())), preferred_element_type=F32)


def kernel(
    nz, ny, nx,
    q_hbm, k_hbm, v_hbm, w_hbm, up_hbm,
    out_ref, qg_ref, kg_ref, vg_ref, wg_ref,
    q, k, v, w, upf, upt, upr,
    terms, others, ssend, srow, zsend, zbuf, tsend, trow, give, state,
    wts, att, normed, scale, hidden, hg, ag, kacc, vacc,
    hsend, hrow, wsend, wrow, wrel, wfar, wout, osend, orel, orecv, oown,
    in_sem, w_sem, ups_sem, upr_sem, rls_sem, rlr_sem, ys_sem, yr_sem,
    xgs_sem, xgr_sem, pfs_sem, pfr_sem,
    ts_sem, tr_sem, gs_sem, gr_sem, s1s, s1r, s2s, s2r, s3s, s3r, hs_sem, hr_sem, ws_sem, wr_sem, os_sem, or_sem,
):
    rows = 2 * ny
    heads = q.shape[1] // HEAD_DIM
    width = q.shape[1]
    tokens = q.shape[0]
    dx = up_hbm.shape[1]
    sl = width // rows
    pieces = HEAD_DIM // sl
    own = heads // 2
    zper = dx // (ny * 128)
    half = width // 2

    s_me = lax.axis_index("seq")
    x_me = lax.axis_index("head")
    z_me = s_me // rows
    r_me = s_me % rows
    y_me = r_me // 2
    c_me = r_me % 2
    x_up = (x_me + 1) % nx
    x_down = (x_me + nx - 1) % nx
    x_far = (x_me + 2) % nx
    partner = (z_me * rows + y_me * 2 + 1 - c_me, x_me)

    def at_row(r):
        return (z_me * rows + r, x_me)

    def at_z(z):
        return (z * rows + r_me, x_me)

    def at_x(x):
        return (s_me, x)

    waits = []

    def send(src, dst, ssem, rsem, device):
        copy = pltpu.make_async_remote_copy(
            src_ref=src, dst_ref=dst, send_sem=ssem, recv_sem=rsem,
            device_id=device, device_id_type=MESH,
        )
        copy.start()
        waits.append(copy)
        return copy

    loads = [
        pltpu.make_async_copy(src, dst, in_sem.at[i])
        for i, (src, dst) in enumerate(
            ((k_hbm, k), (v_hbm, v), (q_hbm, q), (up_hbm, upf.at[x_me]))
        )
    ]
    w_loads = [
        pltpu.make_async_copy(w_hbm.at[:, pl.ds(j * dx, dx)], w.at[j], w_sem.at[j])
        for j in range(nx)
    ]
    for copy in loads + w_loads:
        copy.start()

    barrier = pltpu.get_barrier_semaphore()
    for j in range(1, nz):
        pl.semaphore_signal(barrier, inc=1, device_id=at_z((z_me + j) % nz), device_id_type=MESH)
    for j in range(1, rows):
        pl.semaphore_signal(barrier, inc=1, device_id=at_row((r_me + j) % rows), device_id_type=MESH)
    for j in range(1, nx):
        pl.semaphore_signal(barrier, inc=1, device_id=at_x((x_me + j) % nx), device_id_type=MESH)

    def lanes(h):
        return slice(h * HEAD_DIM, (h + 1) * HEAD_DIM)

    def span(p):
        return slice(p * SPAN, (p + 1) * SPAN)

    def put_terms(which, p, h, term):
        terms[which, h, p] = term.astype(BF16)

    def swap_terms(which):
        return send(
            terms.at[which, pl.ds((1 - c_me) * own, own)], others.at[which],
            ts_sem.at[which], tr_sem.at[which], partner,
        )

    def exchange_slices(which, src, into, ssem, rsem):
        copies = []
        for j in (2, 1, 3):
            peer = (y_me + j) % ny
            copies.append(send(
                src.at[which, peer], into.at[which, y_me],
                ssem.at[which, j], rsem.at[which, j], at_row(peer * 2 + c_me),
            ))
        into[which, y_me] = src[which, y_me]
        return copies

    def chip_terms(which, copy):
        copy.wait_recv()
        for y in range(ny):
            h, at = y // pieces, y % pieces * sl
            for p in range(2):
                ssend[which, y, p] = (
                    terms[which, c_me * own + h, p, at:at + sl].astype(F32)
                    + others[which, h, p, at:at + sl].astype(F32)
                ).astype(BF16)
        return exchange_slices(which, ssend, srow, s1s, s1r)

    def row_sums(which, first, copies):
        for copy in copies:
            copy.wait_recv()
        low = srow[which, 0, first].astype(F32)
        high = srow[which, 0, 1 - first].astype(F32)
        for y in range(1, ny):
            low = low + srow[which, y, first].astype(F32)
            high = high + srow[which, y, 1 - first].astype(F32)
        zsend[which, 0] = low.astype(BF16)
        zsend[which, 1] = (low + high).astype(BF16)
        zbuf[which, z_me] = low.astype(BF16)
        return [
            send(
                zsend.at[which, (z_me + j) // nz], zbuf.at[which, z_me],
                s2s.at[which, j], s2r.at[which, j], at_z((z_me + j) % nz),
            )
            for j in range(1, nz)
        ]

    def prefixes(which, first, copies):
        for copy in copies:
            copy.wait_recv()
        below = jnp.zeros((sl, HEAD_DIM), F32)
        total = jnp.zeros((sl, HEAD_DIM), F32)
        for j in range(nz):
            term = zbuf[which, j].astype(F32)
            total = total + term
            below = below + jnp.where(j < z_me, term, 0.0)
        for y in range(ny):
            tsend[which, y, first] = below.astype(BF16)
            below = below + srow[which, y, first].astype(F32)
        for y in range(ny - 1, -1, -1):
            tsend[which, y, 1 - first] = total.astype(BF16)
            total = total + srow[which, y, 1 - first].astype(F32)
        return exchange_slices(which, tsend, trow, s3s, s3r)

    def give_states(which, first, copies):
        for copy in copies:
            copy.wait_recv()
        for y in range(ny):
            h, at = y // pieces, y % pieces * sl
            for p in range(2):
                before = (c_me == 0) if p == first else (c_me == 1)
                chip = trow[which, y, p].astype(F32)
                mine = terms[which, c_me * own + h, p, at:at + sl].astype(F32)
                give[which, h, p, at:at + sl] = (chip + jnp.where(before, mine, 0.0)).astype(BF16)
        copy = send(
            give.at[which], state.at[which, pl.ds(c_me * own, own)],
            gs_sem.at[which], gr_sem.at[which], partner,
        )
        for y in range(ny):
            h, at = y // pieces, y % pieces * sl
            for p in range(2):
                before = (c_me == 0) if p == first else (c_me == 1)
                chip = trow[which, y, p].astype(F32)
                theirs = others[which, h, p, at:at + sl].astype(F32)
                state[which, c_me * own + h, p, at:at + sl] = (
                    chip + jnp.where(before, 0.0, theirs)
                ).astype(BF16)
        return copy

    def state_of(which, p, h):
        return state[which, h, p]

    loads[0].wait()
    loads[1].wait()
    for h in range(heads):
        for p in range(2):
            put_terms(0, p, h, tn(k[span(p), lanes(h)], v[span(p), lanes(h)]))
    pl.semaphore_wait(barrier, rows + nz + nx - 3)

    swapped = swap_terms(0)
    from_down = send(up_hbm, upf.at[x_me], ups_sem.at[0], upr_sem.at[0], at_x(x_up))
    from_up = send(up_hbm, upf.at[x_me], ups_sem.at[1], upr_sem.at[1], at_x(x_down))

    step1 = chip_terms(0, swapped)

    loads[3].wait()
    def columns_over_y(slot, turn):
        for b in range(zper):
            for yy in range(ny):
                at = (b * ny + yy) * 128
                upt[turn, yy, b] = jnp.transpose(upf[slot, :, at:at + 128].astype(F32)).astype(BF16)
        upr[c_me, slot, y_me] = upt[turn, y_me]
        copies = []
        for m in range(1, ny):
            peer = (y_me + m) % ny
            copies.append(send(
                upt.at[turn, peer], upr.at[c_me, slot, y_me],
                ys_sem.at[turn, m], yr_sem.at[turn, m], at_row(peer * 2 + c_me),
            ))
        return copies

    over_y = columns_over_y(x_me, 0)

    loads[2].wait()
    row_i = lax.broadcasted_iota(jnp.int32, (2 * SPAN, 2 * SPAN), 0)
    col_i = lax.broadcasted_iota(jnp.int32, (2 * SPAN, 2 * SPAN), 1)
    mask = (row_i >= col_i) & ((row_i < SPAN) | (col_i >= SPAN))
    for h in range(heads):
        weights = jnp.where(mask, nt(q[:, lanes(h)], k[:, lanes(h)]), 0.0).astype(BF16)
        wts[h] = weights
        att[:, lanes(h)] = nn(weights, v[:, lanes(h)])

    step2 = row_sums(0, 0, step1)

    for copy in w_loads:
        copy.wait()
    hg[...] = nt(upf[x_me], w[x_me])
    for copy in over_y:
        copy.wait_recv()
    from_down.wait_recv()
    low_half = send(
        upf.at[x_down, pl.ds(0, tokens // 2)], upf.at[x_down, pl.ds(0, tokens // 2)],
        rls_sem.at[0], rlr_sem.at[0], at_x(x_up),
    )
    from_up.wait_recv()
    high_half = send(
        upf.at[x_up, pl.ds(tokens // 2, tokens // 2)], upf.at[x_up, pl.ds(tokens // 2, tokens // 2)],
        rls_sem.at[1], rlr_sem.at[1], at_x(x_down),
    )
    cols_down = send(upr.at[c_me, x_me], upr.at[c_me, x_me], xgs_sem.at[0], xgr_sem.at[0], at_x(x_up))
    cols_up = send(upr.at[c_me, x_me], upr.at[c_me, x_me], xgs_sem.at[1], xgr_sem.at[1], at_x(x_down))
    to_partner = [send(upr.at[c_me, x_me], upr.at[c_me, x_me], pfs_sem.at[0], pfr_sem.at[0], partner)]
    hg[...] = hg[...] + nt(upf[x_down], w[x_down])
    hg[...] = hg[...] + nt(upf[x_up], w[x_up])

    step3 = prefixes(0, 0, step2)

    given = give_states(0, 0, step3)
    low_half.wait_recv()
    high_half.wait_recv()
    far_y = columns_over_y(x_far, 1)
    hg[...] = hg[...] + nt(upf[x_far], w[x_far])
    given.wait_recv()
    for h in range(heads):
        local = att[:, lanes(h)] + jnp.concatenate(
            [nn(q[span(p), lanes(h)], state_of(0, p, h)) for p in range(2)], axis=0
        )
        deviation = jnp.sqrt(jnp.mean(local * local, axis=-1, keepdims=True) + EPS)
        unit = local / deviation
        normed[:, lanes(h)] = unit
        scale[:, lanes(h)] = jnp.broadcast_to(deviation, (2 * SPAN, HEAD_DIM))
        hidden[:, lanes(h)] = unit.astype(BF16)
        hsend[lanes(h), :] = jnp.transpose(unit).astype(BF16)

    y_up = (y_me + 1) % ny
    y_down = (y_me + ny - 1) % ny
    for c in range(2):
        part = hsend.at[pl.ds(c * half, half)]
        send(part, hrow.at[r_me], hs_sem.at[0, c], hr_sem.at[0, c_me], at_row(y_up * 2 + c))
        send(part, hrow.at[r_me], hs_sem.at[1, c], hr_sem.at[1, c_me], at_row(y_down * 2 + c))
    from_partner = send(
        hsend.at[pl.ds(pl.multiple_of((1 - c_me) * half, 128), half)], hrow.at[r_me],
        hs_sem.at[3, 0], hr_sem.at[3, 0], partner,
    )
    hrow[r_me] = hsend[pl.ds(pl.multiple_of(c_me * half, 128), half)]

    for h in range(heads):
        unit = normed[:, lanes(h)]
        grad = hg[:, lanes(h)]
        inner = jnp.mean(grad * unit, axis=-1, keepdims=True)
        attn = ((grad - unit * inner) / scale[:, lanes(h)]).astype(BF16)
        ag[:, lanes(h)] = attn
        for p in range(2):
            put_terms(1, p, h, tn(q[span(p), lanes(h)], attn[span(p)]))
    swapped = swap_terms(1)

    mid = tokens // 2
    osend[0] = nn(hidden[...], w[x_far]).astype(BF16)
    out_low = send(osend.at[0, pl.ds(0, mid)], orel.at[0], os_sem.at[0], or_sem.at[0], at_x(x_up))
    out_high = send(osend.at[0, pl.ds(mid, mid)], orel.at[1], os_sem.at[1], or_sem.at[1], at_x(x_down))
    back1 = chip_terms(1, swapped)
    osend[1] = nn(hidden[...], w[x_up]).astype(BF16)
    over_x = [send(
        osend.at[1, pl.ds(mid, mid)], orecv.at[0, pl.ds(mid, mid)],
        os_sem.at[2], or_sem.at[2], at_x(x_up),
    )]
    osend[2] = nn(hidden[...], w[x_down]).astype(BF16)
    over_x.append(send(
        osend.at[2, pl.ds(0, mid)], orecv.at[1, pl.ds(0, mid)],
        os_sem.at[3], or_sem.at[3], at_x(x_down),
    ))

    cols_down.wait_recv()
    cols_up.wait_recv()
    for i, slot in enumerate((x_down, x_up)):
        to_partner.append(send(
            upr.at[c_me, slot], upr.at[c_me, slot], pfs_sem.at[1 + i], pfr_sem.at[1 + i], partner,
        ))
    for copy in far_y:
        copy.wait_recv()
    to_partner.append(send(
        upr.at[c_me, x_far], upr.at[c_me, x_far], pfs_sem.at[3], pfr_sem.at[3], partner,
    ))

    oown[...] = nn(hidden[...], w[x_me])
    for h in range(heads):
        attn = ag[:, lanes(h)]
        diffs = jnp.where(mask, nt(attn, v[:, lanes(h)]), 0.0).astype(BF16)
        qg_ref[:, lanes(h)] = (
            nn(diffs, k[:, lanes(h)])
            + jnp.concatenate([nt(attn[span(p)], state_of(0, p, h)) for p in range(2)], axis=0)
        ).astype(BF16)
        kacc[:, lanes(h)] = tn(diffs, q[:, lanes(h)])
        vacc[:, lanes(h)] = tn(wts[h], attn)

    def arrived(into, sem):
        pltpu.make_async_remote_copy(
            src_ref=into, dst_ref=into, send_sem=hs_sem.at[3, 0], recv_sem=sem,
            device_id=partner, device_id_type=MESH,
        ).wait_recv()

    for c in range(2):
        arrived(hrow.at[y_down * 2 + c], hr_sem.at[0, c])
        arrived(hrow.at[y_up * 2 + c], hr_sem.at[1, c])
    slot = y_down * 2
    far_row = [send(hrow.at[slot], hrow.at[slot], hs_sem.at[2, 0], hr_sem.at[2, 0], at_row(y_up * 2 + c_me))]
    slot = y_up * 2 + 1
    far_row.append(
        send(hrow.at[slot], hrow.at[slot], hs_sem.at[2, 1], hr_sem.at[2, 1], at_row(y_down * 2 + c_me))
    )

    back2 = row_sums(1, 1, back1)

    out_low.wait_recv()
    osend[1, :mid] = (osend[1, :mid].astype(F32) + orel[0].astype(F32)).astype(BF16)
    over_x.append(send(
        osend.at[1, pl.ds(0, mid)], orecv.at[0, pl.ds(0, mid)],
        os_sem.at[4], or_sem.at[4], at_x(x_up),
    ))
    out_high.wait_recv()
    osend[2, mid:] = (osend[2, mid:].astype(F32) + orel[1].astype(F32)).astype(BF16)
    over_x.append(send(
        osend.at[2, pl.ds(mid, mid)], orecv.at[1, pl.ds(mid, mid)],
        os_sem.at[5], or_sem.at[5], at_x(x_down),
    ))

    for copy in far_row + [from_partner] + to_partner:
        copy.wait_recv()
    feats = jnp.concatenate([hrow[r] for r in range(rows)], axis=1)
    for xx in range(nx):
        cols = jnp.concatenate(
            [
                jnp.concatenate([upr[r % 2, xx, r // 2, b] for r in range(rows)], axis=1)
                for b in range(zper)
            ],
            axis=0,
        )
        part = nt(cols, feats).astype(BF16)
        for b in range(zper):
            for c in range(2):
                at = b * 128 + c * 64
                wsend[xx * zper + b, c] = part[at:at + 64]
    def z_at(step):
        return (z_me + step + nz) % nz

    def owner(z, c):
        return (z * rows + y_me * 2 + c, x_me)

    rel_up = send(wsend.at[z_at(3)], wrel.at[0], ws_sem.at[0, 0], wr_sem.at[5, 0], at_z(z_at(1)))
    rel_down = send(wsend.at[z_at(-3)], wrel.at[1], ws_sem.at[0, 1], wr_sem.at[5, 1], at_z(z_at(-1)))
    far_up = send(wsend.at[z_at(4), 0], wfar.at[0], ws_sem.at[1, 0], wr_sem.at[6, 0], at_z(z_at(2)))
    far_down = send(wsend.at[z_at(4), 1], wfar.at[1], ws_sem.at[1, 1], wr_sem.at[6, 1], at_z(z_at(-2)))
    for i, step in enumerate((1, -1)):
        for c in range(2):
            send(
                wsend.at[z_at(step), c], wrow.at[i, c_me],
                ws_sem.at[2 + i, c], wr_sem.at[i, c_me], owner(z_at(step), c),
            )
    swap = send(wsend.at[z_me, 1 - c_me], wrow.at[4, c_me], ws_sem.at[4, 0], wr_sem.at[4, 0], partner)
    wrow[4, c_me] = wsend[z_me, c_me]

    back3 = prefixes(1, 1, back2)

    for copy in (rel_up, rel_down, far_up, far_down):
        copy.wait_recv()
    for i, step in enumerate((2, -2)):
        for c in range(2):
            term = wsend[z_at(step), c].astype(F32) + wrel[i, c].astype(F32)
            if c == i:
                term = term + wfar[i].astype(F32)
            wout[i, c] = term.astype(BF16)
            send(
                wout.at[i, c], wrow.at[2 + i, c_me],
                ws_sem.at[5 + i, c], wr_sem.at[2 + i, c_me], owner(z_at(step), c),
            )

    total = oown[...]
    for copy in over_x:
        copy.wait_recv()
    out_ref[...] = (total + orecv[0].astype(F32) + orecv[1].astype(F32)).astype(BF16)

    give_states(1, 1, back3).wait_recv()
    for h in range(heads):
        later = [state_of(1, p, h) for p in range(2)]
        kg_ref[:, lanes(h)] = (
            kacc[:, lanes(h)]
            + jnp.concatenate([nt(v[span(p), lanes(h)], later[p]) for p in range(2)], axis=0)
        ).astype(BF16)
        vg_ref[:, lanes(h)] = (
            vacc[:, lanes(h)]
            + jnp.concatenate([nn(k[span(p), lanes(h)], later[p]) for p in range(2)], axis=0)
        ).astype(BF16)

    swap.wait_recv()
    for i in range(4):
        for c in range(2):
            arrived(wrow.at[i, c], wr_sem.at[i, c])
    for c in range(2):
        total = wrow[0, c].astype(F32)
        for i in range(1, 5):
            total = total + wrow[i, c].astype(F32)
        wg_ref[:, c * half:(c + 1) * half] = total
    for copy in waits:
        copy.wait_send()


def write_out(*refs):
    count = len(refs) // 2
    sem = refs[-1]
    copies = [
        pltpu.make_async_copy(refs[i], refs[count + i], sem.at[i]) for i in range(count)
    ]
    for copy in copies:
        copy.start()
    for copy in copies:
        copy.wait()


def on_device(queries, keys, values, out_weight, upstream):
    nx = lax.axis_size("head")
    nz, ny = NZ, NY
    rows = 2 * ny
    pair, length, width = queries.shape
    tokens = pair * length
    heads = width // HEAD_DIM
    dx = upstream.shape[2]
    sl = width // rows
    half = width // 2
    zper = dx // (ny * 128)
    flat = lambda a: a.reshape(tokens, a.shape[2])
    vmem = pltpu.VMEM
    dma = lambda *shape: pltpu.SemaphoreType.DMA(shape)
    part = vmem((2, ny, 2, sl, HEAD_DIM), BF16)
    heads_of = lambda n: vmem((2, n, 2, HEAD_DIM, HEAD_DIM), BF16)
    narrow = vmem((tokens, width), BF16)
    wide = vmem((tokens, width), F32)
    scratch = [
        narrow, narrow, narrow,
        vmem((nx, width, dx), BF16),
        vmem((nx, tokens, dx), BF16),
        vmem((2, ny, zper, 128, tokens), BF16),
        vmem((2, nx, ny, zper, 128, tokens), BF16),
        heads_of(heads), heads_of(heads // 2), part, part,
        vmem((2, 2, sl, HEAD_DIM), BF16),
        vmem((2, nz, sl, HEAD_DIM), BF16),
        part, part, heads_of(heads // 2), heads_of(heads),
        vmem((heads, tokens, tokens), BF16),
        wide, wide, wide, narrow, wide, narrow, wide, wide,
        vmem((width, tokens), BF16), vmem((rows, half, tokens), BF16),
        vmem((nz, 2, 64, half), BF16), vmem((5, 2, 64, half), BF16),
        vmem((2, 2, 64, half), BF16), vmem((2, 64, half), BF16), vmem((2, 2, 64, half), BF16),
        vmem((3, tokens, dx), BF16), vmem((2, tokens // 2, dx), BF16),
        vmem((2, tokens, dx), BF16), vmem((tokens, dx), F32),
        dma(4), dma(nx), dma(2), dma(2), dma(2), dma(2), dma(2, ny), dma(2, ny),
        dma(2), dma(2), dma(4), dma(4),
        dma(2), dma(2), dma(2), dma(2),
        dma(2, ny), dma(2, ny), dma(2, nz), dma(2, nz), dma(2, ny), dma(2, ny),
        dma(4, 2), dma(4, 2), dma(7, 2), dma(7, 2), dma(6), dma(6),
    ]
    grad = jax.ShapeDtypeStruct((tokens, width), BF16)
    shapes = (
        jax.ShapeDtypeStruct((tokens, dx), BF16), grad, grad, grad,
        jax.ShapeDtypeStruct((64, width), F32),
    )
    results = pl.pallas_call(
        functools.partial(kernel, nz, ny, nx),
        out_shape=shapes,
        in_specs=[pl.BlockSpec(memory_space=pltpu.HBM)] * 5,
        out_specs=[pl.BlockSpec(memory_space=pltpu.VMEM)] * 5,
        scratch_shapes=scratch,
        compiler_params=pltpu.CompilerParams(
            collective_id=0, has_side_effects=True, vmem_limit_bytes=48 << 20,
        ),
    )(*[pltpu.with_memory_space_constraint(a, pltpu.HBM) for a in (flat(queries), flat(keys), flat(values), out_weight, flat(upstream))])
    out, qg, kg, vg, wg = pl.pallas_call(
        write_out,
        out_shape=shapes,
        in_specs=[pl.BlockSpec(memory_space=pl.ANY)] * 5,
        out_specs=[pl.BlockSpec(memory_space=pltpu.HBM)] * 5,
        scratch_shapes=[dma(5)],
        compiler_params=pltpu.CompilerParams(vmem_limit_bytes=4 << 20),
    )(*results)
    pairs = lambda a: a.reshape(pair, length, a.shape[1])
    return pairs(out), pairs(qg), pairs(kg), pairs(vg), wg.T


def solution(mesh):
    return jax.shard_map(
        on_device,
        mesh=mesh,
        in_specs=(
            P(None, "seq", "head"),
            P(None, "seq", "head"),
            P(None, "seq", "head"),
            P("head", None),
            P(None, "seq", "head"),
        ),
        out_specs=(
            P(None, "seq", "head"),
            P(None, "seq", "head"),
            P(None, "seq", "head"),
            P(None, "seq", "head"),
            P("head", "seq"),
        ),
        check_vma=False,
    )
```

```python
import functools

import jax
import jax.numpy as jnp
from jax import lax
from jax.experimental import pallas as pl
from jax.experimental.pallas import tpu as pltpu
from jax.sharding import PartitionSpec as P

MESH = pl.DeviceIdType.MESH
SPAN = 64
HEAD_DIM = 128
EPS = 1e-06
NZ = 8
NY = 4
F32 = jnp.float32
BF16 = jnp.bfloat16


def nn(a, b):
    return lax.dot_general(a, b, (((1,), (0,)), ((), ())), preferred_element_type=F32)


def nt(a, b):
    return lax.dot_general(a, b, (((1,), (1,)), ((), ())), preferred_element_type=F32)


def tn(a, b):
    return lax.dot_general(a, b, (((0,), (0,)), ((), ())), preferred_element_type=F32)


def kernel(
    nz, ny, nx,
    q_hbm, k_hbm, v_hbm, w_hbm, up_hbm,
    out_ref, qg_ref, kg_ref, vg_ref, wg_ref,
    q, k, v, w, upf, upt, upr,
    terms, others, ssend, srow, zsend, zbuf, tsend, trow, give, state,
    wts, att, normed, scale, hidden, hg, ag, kacc, vacc,
    hsend, hrow, wsend, wrow, wrel, wfar, wout, osend, orel, orecv, oown,
    in_sem, w_sem, ups_sem, upr_sem, rls_sem, rlr_sem, ys_sem, yr_sem,
    xgs_sem, xgr_sem, pfs_sem, pfr_sem,
    ts_sem, tr_sem, gs_sem, gr_sem, s1s, s1r, s2s, s2r, s3s, s3r, hs_sem, hr_sem, ws_sem, wr_sem, os_sem, or_sem,
):
    rows = 2 * ny
    heads = q.shape[1] // HEAD_DIM
    width = q.shape[1]
    tokens = q.shape[0]
    dx = up_hbm.shape[1]
    sl = width // rows
    pieces = HEAD_DIM // sl
    own = heads // 2
    zper = dx // (ny * 128)
    half = width // 2

    s_me = lax.axis_index("seq")
    x_me = lax.axis_index("head")
    z_me = s_me // rows
    r_me = s_me % rows
    y_me = r_me // 2
    c_me = r_me % 2
    x_up = (x_me + 1) % nx
    x_down = (x_me + nx - 1) % nx
    x_far = (x_me + 2) % nx
    partner = (z_me * rows + y_me * 2 + 1 - c_me, x_me)

    def at_row(r):
        return (z_me * rows + r, x_me)

    def at_z(z):
        return (z * rows + r_me, x_me)

    def at_x(x):
        return (s_me, x)

    waits = []

    def send(src, dst, ssem, rsem, device):
        copy = pltpu.make_async_remote_copy(
            src_ref=src, dst_ref=dst, send_sem=ssem, recv_sem=rsem,
            device_id=device, device_id_type=MESH,
        )
        copy.start()
        waits.append(copy)
        return copy

    loads = [
        pltpu.make_async_copy(src, dst, in_sem.at[i])
        for i, (src, dst) in enumerate(
            ((k_hbm, k), (v_hbm, v), (q_hbm, q), (up_hbm, upf.at[x_me]))
        )
    ]
    w_loads = [
        pltpu.make_async_copy(w_hbm.at[:, pl.ds(j * dx, dx)], w.at[j], w_sem.at[j])
        for j in range(nx)
    ]
    for copy in loads + w_loads:
        copy.start()

    barrier = pltpu.get_barrier_semaphore()
    for j in range(1, nz):
        pl.semaphore_signal(barrier, inc=1, device_id=at_z((z_me + j) % nz), device_id_type=MESH)
    for j in range(1, rows):
        pl.semaphore_signal(barrier, inc=1, device_id=at_row((r_me + j) % rows), device_id_type=MESH)
    for j in range(1, nx):
        pl.semaphore_signal(barrier, inc=1, device_id=at_x((x_me + j) % nx), device_id_type=MESH)

    def lanes(h):
        return slice(h * HEAD_DIM, (h + 1) * HEAD_DIM)

    def span(p):
        return slice(p * SPAN, (p + 1) * SPAN)

    def put_terms(which, p, h, term):
        terms[which, h, p] = term.astype(BF16)

    def swap_terms(which):
        return send(
            terms.at[which, pl.ds((1 - c_me) * own, own)], others.at[which],
            ts_sem.at[which], tr_sem.at[which], partner,
        )

    def exchange_slices(which, src, into, ssem, rsem):
        copies = []
        for j in (2, 1, 3):
            peer = (y_me + j) % ny
            copies.append(send(
                src.at[which, peer], into.at[which, y_me],
                ssem.at[which, j], rsem.at[which, j], at_row(peer * 2 + c_me),
            ))
        into[which, y_me] = src[which, y_me]
        return copies

    def chip_terms(which, copy):
        copy.wait_recv()
        for y in range(ny):
            h, at = y // pieces, y % pieces * sl
            for p in range(2):
                ssend[which, y, p] = (
                    terms[which, c_me * own + h, p, at:at + sl].astype(F32)
                    + others[which, h, p, at:at + sl].astype(F32)
                ).astype(BF16)
        return exchange_slices(which, ssend, srow, s1s, s1r)

    def row_sums(which, first, copies):
        for copy in copies:
            copy.wait_recv()
        low = srow[which, 0, first].astype(F32)
        high = srow[which, 0, 1 - first].astype(F32)
        for y in range(1, ny):
            low = low + srow[which, y, first].astype(F32)
            high = high + srow[which, y, 1 - first].astype(F32)
        zsend[which, 0] = low.astype(BF16)
        zsend[which, 1] = (low + high).astype(BF16)
        zbuf[which, z_me] = low.astype(BF16)
        return [
            send(
                zsend.at[which, (z_me + j) // nz], zbuf.at[which, z_me],
                s2s.at[which, j], s2r.at[which, j], at_z((z_me + j) % nz),
            )
            for j in (4, 3, 5, 2, 6, 1, 7)
        ]

    def prefixes(which, first, copies):
        for copy in copies:
            copy.wait_recv()
        below = jnp.zeros((sl, HEAD_DIM), F32)
        total = jnp.zeros((sl, HEAD_DIM), F32)
        for j in range(nz):
            term = zbuf[which, j].astype(F32)
            total = total + term
            below = below + jnp.where(j < z_me, term, 0.0)
        for y in range(ny):
            tsend[which, y, first] = below.astype(BF16)
            below = below + srow[which, y, first].astype(F32)
        for y in range(ny - 1, -1, -1):
            tsend[which, y, 1 - first] = total.astype(BF16)
            total = total + srow[which, y, 1 - first].astype(F32)
        return exchange_slices(which, tsend, trow, s3s, s3r)

    def give_states(which, first, copies):
        for copy in copies:
            copy.wait_recv()
        for y in range(ny):
            h, at = y // pieces, y % pieces * sl
            for p in range(2):
                before = (c_me == 0) if p == first else (c_me == 1)
                chip = trow[which, y, p].astype(F32)
                mine = terms[which, c_me * own + h, p, at:at + sl].astype(F32)
                give[which, h, p, at:at + sl] = (chip + jnp.where(before, mine, 0.0)).astype(BF16)
        copy = send(
            give.at[which], state.at[which, pl.ds(c_me * own, own)],
            gs_sem.at[which], gr_sem.at[which], partner,
        )
        for y in range(ny):
            h, at = y // pieces, y % pieces * sl
            for p in range(2):
                before = (c_me == 0) if p == first else (c_me == 1)
                chip = trow[which, y, p].astype(F32)
                theirs = others[which, h, p, at:at + sl].astype(F32)
                state[which, c_me * own + h, p, at:at + sl] = (
                    chip + jnp.where(before, 0.0, theirs)
                ).astype(BF16)
        return copy

    def state_of(which, p, h):
        return state[which, h, p]

    loads[0].wait()
    loads[1].wait()
    for h in range(heads):
        for p in range(2):
            put_terms(0, p, h, tn(k[span(p), lanes(h)], v[span(p), lanes(h)]))
    pl.semaphore_wait(barrier, rows + nz + nx - 3)

    swapped = swap_terms(0)
    from_down = send(up_hbm, upf.at[x_me], ups_sem.at[0], upr_sem.at[0], at_x(x_up))
    from_up = send(up_hbm, upf.at[x_me], ups_sem.at[1], upr_sem.at[1], at_x(x_down))

    step1 = chip_terms(0, swapped)

    loads[3].wait()
    def columns_over_y(slot, turn):
        for b in range(zper):
            for yy in range(ny):
                at = (b * ny + yy) * 128
                upt[turn, yy, b] = jnp.transpose(upf[slot, :, at:at + 128].astype(F32)).astype(BF16)
        upr[c_me, slot, y_me] = upt[turn, y_me]
        copies = []
        for m in range(1, ny):
            peer = (y_me + m) % ny
            copies.append(send(
                upt.at[turn, peer], upr.at[c_me, slot, y_me],
                ys_sem.at[turn, m], yr_sem.at[turn, m], at_row(peer * 2 + c_me),
            ))
        return copies

    over_y = columns_over_y(x_me, 0)

    loads[2].wait()
    row_i = lax.broadcasted_iota(jnp.int32, (2 * SPAN, 2 * SPAN), 0)
    col_i = lax.broadcasted_iota(jnp.int32, (2 * SPAN, 2 * SPAN), 1)
    mask = (row_i >= col_i) & ((row_i < SPAN) | (col_i >= SPAN))
    for h in range(heads):
        weights = jnp.where(mask, nt(q[:, lanes(h)], k[:, lanes(h)]), 0.0).astype(BF16)
        wts[h] = weights
        att[:, lanes(h)] = nn(weights, v[:, lanes(h)])

    step2 = row_sums(0, 0, step1)

    for copy in w_loads:
        copy.wait()
    hg[...] = nt(upf[x_me], w[x_me])
    for copy in over_y:
        copy.wait_recv()
    from_down.wait_recv()
    low_half = send(
        upf.at[x_down, pl.ds(0, tokens // 2)], upf.at[x_down, pl.ds(0, tokens // 2)],
        rls_sem.at[0], rlr_sem.at[0], at_x(x_up),
    )
    from_up.wait_recv()
    high_half = send(
        upf.at[x_up, pl.ds(tokens // 2, tokens // 2)], upf.at[x_up, pl.ds(tokens // 2, tokens // 2)],
        rls_sem.at[1], rlr_sem.at[1], at_x(x_down),
    )
    cols_down = send(upr.at[c_me, x_me], upr.at[c_me, x_me], xgs_sem.at[0], xgr_sem.at[0], at_x(x_up))
    cols_up = send(upr.at[c_me, x_me], upr.at[c_me, x_me], xgs_sem.at[1], xgr_sem.at[1], at_x(x_down))
    to_partner = [send(upr.at[c_me, x_me], upr.at[c_me, x_me], pfs_sem.at[0], pfr_sem.at[0], partner)]
    hg[...] = hg[...] + nt(upf[x_down], w[x_down])
    hg[...] = hg[...] + nt(upf[x_up], w[x_up])

    step3 = prefixes(0, 0, step2)

    given = give_states(0, 0, step3)
    low_half.wait_recv()
    high_half.wait_recv()
    far_y = columns_over_y(x_far, 1)
    hg[...] = hg[...] + nt(upf[x_far], w[x_far])
    def tile(h):
        return pl.ds(pl.multiple_of(h * HEAD_DIM, HEAD_DIM), HEAD_DIM)

    def hide(h):
        at = tile(h)
        local = att[:, at] + jnp.concatenate(
            [nn(q[span(p), at], state_of(0, p, h)) for p in range(2)], axis=0
        )
        inverse = lax.rsqrt(jnp.mean(local * local, axis=-1, keepdims=True) + EPS)
        unit = local * inverse
        normed[:, at] = unit
        scale[:, at] = jnp.broadcast_to(inverse, (2 * SPAN, HEAD_DIM))
        hidden[:, at] = unit.astype(BF16)
        hsend[at, :] = jnp.transpose(unit).astype(BF16)

    y_up = (y_me + 1) % ny
    y_down = (y_me + ny - 1) % ny

    def hidden_over_y(n, c):
        part = hsend.at[pl.ds(pl.multiple_of(c * half, 128), half)]
        send(part, hrow.at[r_me], hs_sem.at[0, n], hr_sem.at[0, c_me], at_row(y_up * 2 + c))
        send(part, hrow.at[r_me], hs_sem.at[1, n], hr_sem.at[1, c_me], at_row(y_down * 2 + c))

    for i in range(own):
        hide(c_me * own + i)
    hidden_over_y(0, c_me)
    given.wait_recv()
    for i in range(own):
        hide((1 - c_me) * own + i)
    hidden_over_y(1, 1 - c_me)
    from_partner = send(
        hsend.at[pl.ds(pl.multiple_of((1 - c_me) * half, 128), half)], hrow.at[r_me],
        hs_sem.at[3, 0], hr_sem.at[3, 0], partner,
    )
    hrow[r_me] = hsend[pl.ds(pl.multiple_of(c_me * half, 128), half)]

    for i in range(heads):
        h = (1 - i // own) * own + i % own + c_me * (2 * (i // own) - 1) * own
        at = tile(h)
        unit = normed[:, at]
        grad = hg[:, at]
        inner = jnp.mean(grad * unit, axis=-1, keepdims=True)
        attn = ((grad - unit * inner) * scale[:, at]).astype(BF16)
        ag[:, at] = attn
        for p in range(2):
            put_terms(1, p, h, tn(q[span(p), at], attn[span(p)]))
        if i == own - 1:
            swapped = swap_terms(1)

    mid = tokens // 2
    osend[0] = nn(hidden[...], w[x_far]).astype(BF16)
    out_low = send(osend.at[0, pl.ds(0, mid)], orel.at[0], os_sem.at[0], or_sem.at[0], at_x(x_up))
    out_high = send(osend.at[0, pl.ds(mid, mid)], orel.at[1], os_sem.at[1], or_sem.at[1], at_x(x_down))
    back1 = chip_terms(1, swapped)
    osend[1] = nn(hidden[...], w[x_up]).astype(BF16)
    over_x = [send(
        osend.at[1, pl.ds(mid, mid)], orecv.at[0, pl.ds(mid, mid)],
        os_sem.at[2], or_sem.at[2], at_x(x_up),
    )]
    osend[2] = nn(hidden[...], w[x_down]).astype(BF16)
    over_x.append(send(
        osend.at[2, pl.ds(0, mid)], orecv.at[1, pl.ds(0, mid)],
        os_sem.at[3], or_sem.at[3], at_x(x_down),
    ))

    cols_down.wait_recv()
    cols_up.wait_recv()
    for i, slot in enumerate((x_down, x_up)):
        to_partner.append(send(
            upr.at[c_me, slot], upr.at[c_me, slot], pfs_sem.at[1 + i], pfr_sem.at[1 + i], partner,
        ))
    for copy in far_y:
        copy.wait_recv()
    to_partner.append(send(
        upr.at[c_me, x_far], upr.at[c_me, x_far], pfs_sem.at[3], pfr_sem.at[3], partner,
    ))

    oown[...] = nn(hidden[...], w[x_me])
    for h in range(heads):
        attn = ag[:, lanes(h)]
        diffs = jnp.where(mask, nt(attn, v[:, lanes(h)]), 0.0).astype(BF16)
        qg_ref[:, lanes(h)] = (
            nn(diffs, k[:, lanes(h)])
            + jnp.concatenate([nt(attn[span(p)], state_of(0, p, h)) for p in range(2)], axis=0)
        ).astype(BF16)
        kacc[:, lanes(h)] = tn(diffs, q[:, lanes(h)])
        vacc[:, lanes(h)] = tn(wts[h], attn)

    def arrived(into, sem):
        pltpu.make_async_remote_copy(
            src_ref=into, dst_ref=into, send_sem=hs_sem.at[3, 0], recv_sem=sem,
            device_id=partner, device_id_type=MESH,
        ).wait_recv()

    slot = y_down * 2
    arrived(hrow.at[slot], hr_sem.at[0, 0])
    far_row = [send(hrow.at[slot], hrow.at[slot], hs_sem.at[2, 0], hr_sem.at[2, 0], at_row(y_up * 2 + c_me))]
    slot = y_up * 2 + 1
    arrived(hrow.at[slot], hr_sem.at[1, 1])
    far_row.append(
        send(hrow.at[slot], hrow.at[slot], hs_sem.at[2, 1], hr_sem.at[2, 1], at_row(y_down * 2 + c_me))
    )

    back2 = row_sums(1, 1, back1)

    out_low.wait_recv()
    osend[1, :mid] = (osend[1, :mid].astype(F32) + orel[0].astype(F32)).astype(BF16)
    over_x.append(send(
        osend.at[1, pl.ds(0, mid)], orecv.at[0, pl.ds(0, mid)],
        os_sem.at[4], or_sem.at[4], at_x(x_up),
    ))
    out_high.wait_recv()
    osend[2, mid:] = (osend[2, mid:].astype(F32) + orel[1].astype(F32)).astype(BF16)
    over_x.append(send(
        osend.at[2, pl.ds(mid, mid)], orecv.at[1, pl.ds(mid, mid)],
        os_sem.at[5], or_sem.at[5], at_x(x_down),
    ))

    arrived(hrow.at[y_down * 2 + 1], hr_sem.at[0, 1])
    arrived(hrow.at[y_up * 2], hr_sem.at[1, 0])
    for copy in far_row + [from_partner] + to_partner:
        copy.wait_recv()
    feats = jnp.concatenate([hrow[r] for r in range(rows)], axis=1)
    def z_at(step):
        return (z_me + step + nz) % nz

    def owner(z, c):
        return (z * rows + y_me * 2 + c, x_me)

    first_x = (z_at(3) // zper)
    for n in range(nx):
        xx = (first_x + n) % nx
        cols = jnp.concatenate(
            [
                jnp.concatenate([upr[r % 2, xx, r // 2, b] for r in range(rows)], axis=1)
                for b in range(zper)
            ],
            axis=0,
        )
        part = nt(cols, feats).astype(BF16)
        for b in range(zper):
            for c in range(2):
                at = b * 128 + c * 64
                wsend[xx * zper + b, c] = part[at:at + 64]
        if n == 1:
            rel_up = send(wsend.at[z_at(3)], wrel.at[0], ws_sem.at[0, 0], wr_sem.at[5, 0], at_z(z_at(1)))
            rel_down = send(wsend.at[z_at(-3)], wrel.at[1], ws_sem.at[0, 1], wr_sem.at[5, 1], at_z(z_at(-1)))
            far_up = send(wsend.at[z_at(4), 0], wfar.at[0], ws_sem.at[1, 0], wr_sem.at[6, 0], at_z(z_at(2)))
            far_down = send(wsend.at[z_at(4), 1], wfar.at[1], ws_sem.at[1, 1], wr_sem.at[6, 1], at_z(z_at(-2)))
    for i, step in enumerate((1, -1)):
        for c in range(2):
            send(
                wsend.at[z_at(step), c], wrow.at[i, c_me],
                ws_sem.at[2 + i, c], wr_sem.at[i, c_me], owner(z_at(step), c),
            )
    swap = send(wsend.at[z_me, 1 - c_me], wrow.at[4, c_me], ws_sem.at[4, 0], wr_sem.at[4, 0], partner)
    wrow[4, c_me] = wsend[z_me, c_me]

    back3 = prefixes(1, 1, back2)

    for i, step in enumerate((2, -2)):
        for copy in ((rel_up, far_up), (rel_down, far_down))[i]:
            copy.wait_recv()
        for c in range(2):
            term = wsend[z_at(step), c].astype(F32) + wrel[i, c].astype(F32)
            if c == i:
                term = term + wfar[i].astype(F32)
            wout[i, c] = term.astype(BF16)
            send(
                wout.at[i, c], wrow.at[2 + i, c_me],
                ws_sem.at[5 + i, c], wr_sem.at[2 + i, c_me], owner(z_at(step), c),
            )

    total = oown[...]
    for copy in over_x:
        copy.wait_recv()
    out_ref[...] = (total + orecv[0].astype(F32) + orecv[1].astype(F32)).astype(BF16)

    given = give_states(1, 1, back3)
    for i in range(heads):
        if i == own:
            given.wait_recv()
        h = (i // own) * own + i % own + c_me * (1 - 2 * (i // own)) * own
        at = tile(h)
        later = [state_of(1, p, h) for p in range(2)]
        kg_ref[:, at] = (
            kacc[:, at]
            + jnp.concatenate([nt(v[span(p), at], later[p]) for p in range(2)], axis=0)
        ).astype(BF16)
        vg_ref[:, at] = (
            vacc[:, at]
            + jnp.concatenate([nn(k[span(p), at], later[p]) for p in range(2)], axis=0)
        ).astype(BF16)

    swap.wait_recv()
    for i in range(4):
        for c in range(2):
            arrived(wrow.at[i, c], wr_sem.at[i, c])
    for c in range(2):
        total = wrow[0, c].astype(F32)
        for i in range(1, 5):
            total = total + wrow[i, c].astype(F32)
        wg_ref[:, c * half:(c + 1) * half] = total
    for copy in waits:
        copy.wait_send()


def write_out(*refs):
    count = len(refs) // 2
    sem = refs[-1]
    copies = [
        pltpu.make_async_copy(refs[i], refs[count + i], sem.at[i]) for i in range(count)
    ]
    for copy in copies:
        copy.start()
    for copy in copies:
        copy.wait()


def on_device(queries, keys, values, out_weight, upstream):
    nx = lax.axis_size("head")
    nz, ny = NZ, NY
    rows = 2 * ny
    pair, length, width = queries.shape
    tokens = pair * length
    heads = width // HEAD_DIM
    dx = upstream.shape[2]
    sl = width // rows
    half = width // 2
    zper = dx // (ny * 128)
    flat = lambda a: a.reshape(tokens, a.shape[2])
    vmem = pltpu.VMEM
    dma = lambda *shape: pltpu.SemaphoreType.DMA(shape)
    part = vmem((2, ny, 2, sl, HEAD_DIM), BF16)
    heads_of = lambda n: vmem((2, n, 2, HEAD_DIM, HEAD_DIM), BF16)
    narrow = vmem((tokens, width), BF16)
    wide = vmem((tokens, width), F32)
    scratch = [
        narrow, narrow, narrow,
        vmem((nx, width, dx), BF16),
        vmem((nx, tokens, dx), BF16),
        vmem((2, ny, zper, 128, tokens), BF16),
        vmem((2, nx, ny, zper, 128, tokens), BF16),
        heads_of(heads), heads_of(heads // 2), part, part,
        vmem((2, 2, sl, HEAD_DIM), BF16),
        vmem((2, nz, sl, HEAD_DIM), BF16),
        part, part, heads_of(heads // 2), heads_of(heads),
        vmem((heads, tokens, tokens), BF16),
        wide, wide, wide, narrow, wide, narrow, wide, wide,
        vmem((width, tokens), BF16), vmem((rows, half, tokens), BF16),
        vmem((nz, 2, 64, half), BF16), vmem((5, 2, 64, half), BF16),
        vmem((2, 2, 64, half), BF16), vmem((2, 64, half), BF16), vmem((2, 2, 64, half), BF16),
        vmem((3, tokens, dx), BF16), vmem((2, tokens // 2, dx), BF16),
        vmem((2, tokens, dx), BF16), vmem((tokens, dx), F32),
        dma(4), dma(nx), dma(2), dma(2), dma(2), dma(2), dma(2, ny), dma(2, ny),
        dma(2), dma(2), dma(4), dma(4),
        dma(2), dma(2), dma(2), dma(2),
        dma(2, ny), dma(2, ny), dma(2, nz), dma(2, nz), dma(2, ny), dma(2, ny),
        dma(4, 2), dma(4, 2), dma(7, 2), dma(7, 2), dma(6), dma(6),
    ]
    grad = jax.ShapeDtypeStruct((tokens, width), BF16)
    shapes = (
        jax.ShapeDtypeStruct((tokens, dx), BF16), grad, grad, grad,
        jax.ShapeDtypeStruct((64, width), F32),
    )
    results = pl.pallas_call(
        functools.partial(kernel, nz, ny, nx),
        out_shape=shapes,
        in_specs=[pl.BlockSpec(memory_space=pltpu.HBM)] * 5,
        out_specs=[pl.BlockSpec(memory_space=pltpu.VMEM)] * 5,
        scratch_shapes=scratch,
        compiler_params=pltpu.CompilerParams(
            collective_id=0, has_side_effects=True, vmem_limit_bytes=48 << 20,
        ),
    )(*[pltpu.with_memory_space_constraint(a, pltpu.HBM) for a in (flat(queries), flat(keys), flat(values), out_weight, flat(upstream))])
    out, qg, kg, vg, wg = pl.pallas_call(
        write_out,
        out_shape=shapes,
        in_specs=[pl.BlockSpec(memory_space=pl.ANY)] * 5,
        out_specs=[pl.BlockSpec(memory_space=pltpu.HBM)] * 5,
        scratch_shapes=[dma(5)],
        compiler_params=pltpu.CompilerParams(vmem_limit_bytes=4 << 20),
    )(*results)
    pairs = lambda a: a.reshape(pair, length, a.shape[1])
    return pairs(out), pairs(qg), pairs(kg), pairs(vg), wg.T


def solution(mesh):
    return jax.shard_map(
        on_device,
        mesh=mesh,
        in_specs=(
            P(None, "seq", "head"),
            P(None, "seq", "head"),
            P(None, "seq", "head"),
            P("head", None),
            P(None, "seq", "head"),
        ),
        out_specs=(
            P(None, "seq", "head"),
            P(None, "seq", "head"),
            P(None, "seq", "head"),
            P(None, "seq", "head"),
            P("head", "seq"),
        ),
        check_vma=False,
    )
```

```python
import functools

import jax
import jax.numpy as jnp
from jax import lax
from jax.experimental import pallas as pl
from jax.experimental.pallas import tpu as pltpu
from jax.sharding import PartitionSpec as P

MESH = pl.DeviceIdType.MESH
SPAN = 64
HEAD_DIM = 128
EPS = 1e-06
NZ = 8
NY = 4
F32 = jnp.float32
BF16 = jnp.bfloat16


def nn(a, b):
    return lax.dot_general(a, b, (((1,), (0,)), ((), ())), preferred_element_type=F32)


def nt(a, b):
    return lax.dot_general(a, b, (((1,), (1,)), ((), ())), preferred_element_type=F32)


def tn(a, b):
    return lax.dot_general(a, b, (((0,), (0,)), ((), ())), preferred_element_type=F32)


def kernel(
    nz, ny, nx,
    q_hbm, k_hbm, v_hbm, w_hbm, up_hbm,
    out_ref, qg_ref, kg_ref, vg_ref, wg_ref,
    q, k, v, w, upf, upt, upr,
    terms, others, ssend, srow, zsend, zbuf, tsend, trow, give, state,
    wts, att, normed, scale, hidden, hg, ag, kacc, vacc,
    hsend, hrow, wsend, wrow, wrel, wfar, wout, osend, orel, orecv, oown,
    in_sem, w_sem, ups_sem, upr_sem, rls_sem, rlr_sem, ys_sem, yr_sem,
    xgs_sem, xgr_sem, pfs_sem, pfr_sem,
    ts_sem, tr_sem, gs_sem, gr_sem, s1s, s1r, s2s, s2r, s3s, s3r, hs_sem, hr_sem, ws_sem, wr_sem, os_sem, or_sem,
):
    rows = 2 * ny
    heads = q.shape[1] // HEAD_DIM
    width = q.shape[1]
    tokens = q.shape[0]
    dx = up_hbm.shape[1]
    sl = width // rows
    pieces = HEAD_DIM // sl
    own = heads // 2
    zper = dx // (ny * 128)
    half = width // 2

    s_me = lax.axis_index("seq")
    x_me = lax.axis_index("head")
    z_me = s_me // rows
    r_me = s_me % rows
    y_me = r_me // 2
    c_me = r_me % 2
    x_up = (x_me + 1) % nx
    x_down = (x_me + nx - 1) % nx
    x_far = (x_me + 2) % nx
    partner = (z_me * rows + y_me * 2 + 1 - c_me, x_me)

    def at_row(r):
        return (z_me * rows + r, x_me)

    def at_z(z):
        return (z * rows + r_me, x_me)

    def at_x(x):
        return (s_me, x)

    waits = []

    def send(src, dst, ssem, rsem, device):
        copy = pltpu.make_async_remote_copy(
            src_ref=src, dst_ref=dst, send_sem=ssem, recv_sem=rsem,
            device_id=device, device_id_type=MESH,
        )
        copy.start()
        waits.append(copy)
        return copy

    loads = [
        pltpu.make_async_copy(src, dst, in_sem.at[i])
        for i, (src, dst) in enumerate(
            ((k_hbm, k), (v_hbm, v), (q_hbm, q), (up_hbm, upf.at[x_me]))
        )
    ]
    w_loads = [
        pltpu.make_async_copy(w_hbm.at[:, pl.ds(j * dx, dx)], w.at[j], w_sem.at[j])
        for j in range(nx)
    ]
    for copy in loads + w_loads:
        copy.start()

    barrier = pltpu.get_barrier_semaphore()
    for j in range(1, nz):
        pl.semaphore_signal(barrier, inc=1, device_id=at_z((z_me + j) % nz), device_id_type=MESH)
    for j in range(1, rows):
        pl.semaphore_signal(barrier, inc=1, device_id=at_row((r_me + j) % rows), device_id_type=MESH)
    for j in range(1, nx):
        pl.semaphore_signal(barrier, inc=1, device_id=at_x((x_me + j) % nx), device_id_type=MESH)

    def lanes(h):
        return slice(h * HEAD_DIM, (h + 1) * HEAD_DIM)

    def span(p):
        return slice(p * SPAN, (p + 1) * SPAN)

    def put_terms(which, p, h, term):
        terms[which, h, p] = term.astype(BF16)

    def swap_terms(which):
        return send(
            terms.at[which, pl.ds((1 - c_me) * own, own)], others.at[which],
            ts_sem.at[which], tr_sem.at[which], partner,
        )

    def exchange_slices(which, src, into, ssem, rsem):
        copies = []
        for j in (2, 1, 3):
            peer = (y_me + j) % ny
            copies.append(send(
                src.at[which, peer], into.at[which, y_me],
                ssem.at[which, j], rsem.at[which, j], at_row(peer * 2 + c_me),
            ))
        into[which, y_me] = src[which, y_me]
        return copies

    def chip_terms(which, copy):
        copy.wait_recv()
        for y in range(ny):
            h, at = y // pieces, y % pieces * sl
            for p in range(2):
                ssend[which, y, p] = (
                    terms[which, c_me * own + h, p, at:at + sl].astype(F32)
                    + others[which, h, p, at:at + sl].astype(F32)
                ).astype(BF16)
        return exchange_slices(which, ssend, srow, s1s, s1r)

    def row_sums(which, first, copies):
        for copy in copies:
            copy.wait_recv()
        low = srow[which, 0, first].astype(F32)
        high = srow[which, 0, 1 - first].astype(F32)
        for y in range(1, ny):
            low = low + srow[which, y, first].astype(F32)
            high = high + srow[which, y, 1 - first].astype(F32)
        zsend[which, 0] = low.astype(BF16)
        zsend[which, 1] = (low + high).astype(BF16)
        zbuf[which, z_me] = low.astype(BF16)
        return [
            send(
                zsend.at[which, (z_me + j) // nz], zbuf.at[which, z_me],
                s2s.at[which, j], s2r.at[which, j], at_z((z_me + j) % nz),
            )
            for j in (4, 3, 5, 2, 6, 1, 7)
        ]

    def prefixes(which, first, copies):
        for copy in copies:
            copy.wait_recv()
        below = jnp.zeros((sl, HEAD_DIM), F32)
        total = jnp.zeros((sl, HEAD_DIM), F32)
        for j in range(nz):
            term = zbuf[which, j].astype(F32)
            total = total + term
            below = below + jnp.where(j < z_me, term, 0.0)
        for y in range(ny):
            tsend[which, y, first] = below.astype(BF16)
            below = below + srow[which, y, first].astype(F32)
        for y in range(ny - 1, -1, -1):
            tsend[which, y, 1 - first] = total.astype(BF16)
            total = total + srow[which, y, 1 - first].astype(F32)
        return exchange_slices(which, tsend, trow, s3s, s3r)

    def give_states(which, first, copies):
        for copy in copies:
            copy.wait_recv()
        for y in range(ny):
            h, at = y // pieces, y % pieces * sl
            for p in range(2):
                before = (c_me == 0) if p == first else (c_me == 1)
                chip = trow[which, y, p].astype(F32)
                mine = terms[which, c_me * own + h, p, at:at + sl].astype(F32)
                give[which, h, p, at:at + sl] = (chip + jnp.where(before, mine, 0.0)).astype(BF16)
        copy = send(
            give.at[which], state.at[which, pl.ds(c_me * own, own)],
            gs_sem.at[which], gr_sem.at[which], partner,
        )
        for y in range(ny):
            h, at = y // pieces, y % pieces * sl
            for p in range(2):
                before = (c_me == 0) if p == first else (c_me == 1)
                chip = trow[which, y, p].astype(F32)
                theirs = others[which, h, p, at:at + sl].astype(F32)
                state[which, c_me * own + h, p, at:at + sl] = (
                    chip + jnp.where(before, 0.0, theirs)
                ).astype(BF16)
        return copy

    def state_of(which, p, h):
        return state[which, h, p]

    loads[0].wait()
    loads[1].wait()
    for h in range(heads):
        for p in range(2):
            put_terms(0, p, h, tn(k[span(p), lanes(h)], v[span(p), lanes(h)]))
    pl.semaphore_wait(barrier, rows + nz + nx - 3)

    swapped = swap_terms(0)
    from_down = send(up_hbm, upf.at[x_me], ups_sem.at[0], upr_sem.at[0], at_x(x_up))
    from_up = send(up_hbm, upf.at[x_me], ups_sem.at[1], upr_sem.at[1], at_x(x_down))

    step1 = chip_terms(0, swapped)

    loads[3].wait()
    def columns_over_y(slot, turn):
        for b in range(zper):
            for yy in range(ny):
                at = (b * ny + yy) * 128
                upt[turn, yy, b] = jnp.transpose(upf[slot, :, at:at + 128].astype(F32)).astype(BF16)
        upr[c_me, slot, y_me] = upt[turn, y_me]
        copies = []
        for m in range(1, ny):
            peer = (y_me + m) % ny
            copies.append(send(
                upt.at[turn, peer], upr.at[c_me, slot, y_me],
                ys_sem.at[turn, m], yr_sem.at[turn, m], at_row(peer * 2 + c_me),
            ))
        return copies

    over_y = columns_over_y(x_me, 0)

    loads[2].wait()
    row_i = lax.broadcasted_iota(jnp.int32, (2 * SPAN, 2 * SPAN), 0)
    col_i = lax.broadcasted_iota(jnp.int32, (2 * SPAN, 2 * SPAN), 1)
    mask = (row_i >= col_i) & ((row_i < SPAN) | (col_i >= SPAN))
    for h in range(heads):
        weights = jnp.where(mask, nt(q[:, lanes(h)], k[:, lanes(h)]), 0.0).astype(BF16)
        wts[h] = weights
        att[:, lanes(h)] = nn(weights, v[:, lanes(h)])

    step2 = row_sums(0, 0, step1)

    for copy in w_loads:
        copy.wait()
    hg[...] = nt(upf[x_me], w[x_me])
    for copy in over_y:
        copy.wait_recv()
    from_down.wait_recv()
    low_half = send(
        upf.at[x_down, pl.ds(0, tokens // 2)], upf.at[x_down, pl.ds(0, tokens // 2)],
        rls_sem.at[0], rlr_sem.at[0], at_x(x_up),
    )
    from_up.wait_recv()
    high_half = send(
        upf.at[x_up, pl.ds(tokens // 2, tokens // 2)], upf.at[x_up, pl.ds(tokens // 2, tokens // 2)],
        rls_sem.at[1], rlr_sem.at[1], at_x(x_down),
    )
    cols_down = send(upr.at[c_me, x_me], upr.at[c_me, x_me], xgs_sem.at[0], xgr_sem.at[0], at_x(x_up))
    cols_up = send(upr.at[c_me, x_me], upr.at[c_me, x_me], xgs_sem.at[1], xgr_sem.at[1], at_x(x_down))
    to_partner = [send(upr.at[c_me, x_me], upr.at[c_me, x_me], pfs_sem.at[0], pfr_sem.at[0], partner)]
    hg[...] = hg[...] + nt(upf[x_down], w[x_down])
    hg[...] = hg[...] + nt(upf[x_up], w[x_up])

    step3 = prefixes(0, 0, step2)

    given = give_states(0, 0, step3)
    low_half.wait_recv()
    high_half.wait_recv()
    far_y = columns_over_y(x_far, 1)
    hg[...] = hg[...] + nt(upf[x_far], w[x_far])
    def tile(h):
        return pl.ds(pl.multiple_of(h * HEAD_DIM, HEAD_DIM), HEAD_DIM)

    def hide(h):
        at = tile(h)
        local = att[:, at] + jnp.concatenate(
            [nn(q[span(p), at], state_of(0, p, h)) for p in range(2)], axis=0
        )
        inverse = lax.rsqrt(jnp.mean(local * local, axis=-1, keepdims=True) + EPS)
        unit = local * inverse
        normed[:, at] = unit
        scale[:, at] = jnp.broadcast_to(inverse, (2 * SPAN, HEAD_DIM))
        hidden[:, at] = unit.astype(BF16)
        hsend[at, :] = jnp.transpose(unit).astype(BF16)

    y_up = (y_me + 1) % ny
    y_down = (y_me + ny - 1) % ny

    def hidden_over_y(n, c):
        part = hsend.at[pl.ds(pl.multiple_of(c * half, 128), half)]
        send(part, hrow.at[r_me], hs_sem.at[0, n], hr_sem.at[0, c_me], at_row(y_up * 2 + c))
        send(part, hrow.at[r_me], hs_sem.at[1, n], hr_sem.at[1, c_me], at_row(y_down * 2 + c))

    for i in range(own):
        hide(c_me * own + i)
    hidden_over_y(0, c_me)
    given.wait_recv()
    for i in range(own):
        hide((1 - c_me) * own + i)
    hidden_over_y(1, 1 - c_me)
    from_partner = send(
        hsend.at[pl.ds(pl.multiple_of((1 - c_me) * half, 128), half)], hrow.at[r_me],
        hs_sem.at[3, 0], hr_sem.at[3, 0], partner,
    )
    hrow[r_me] = hsend[pl.ds(pl.multiple_of(c_me * half, 128), half)]

    for i in range(heads):
        h = (1 - i // own) * own + i % own + c_me * (2 * (i // own) - 1) * own
        at = tile(h)
        unit = normed[:, at]
        grad = hg[:, at]
        inner = jnp.mean(grad * unit, axis=-1, keepdims=True)
        attn = ((grad - unit * inner) * scale[:, at]).astype(BF16)
        ag[:, at] = attn
        for p in range(2):
            put_terms(1, p, h, tn(q[span(p), at], attn[span(p)]))
        if i == own - 1:
            swapped = swap_terms(1)

    mid = tokens // 2
    osend[0] = nn(hidden[...], w[x_far]).astype(BF16)
    out_low = send(osend.at[0, pl.ds(0, mid)], orel.at[0], os_sem.at[0], or_sem.at[0], at_x(x_up))
    out_high = send(osend.at[0, pl.ds(mid, mid)], orel.at[1], os_sem.at[1], or_sem.at[1], at_x(x_down))
    back1 = chip_terms(1, swapped)
    osend[1] = nn(hidden[...], w[x_up]).astype(BF16)
    over_x = [send(
        osend.at[1, pl.ds(mid, mid)], orecv.at[0, pl.ds(mid, mid)],
        os_sem.at[2], or_sem.at[2], at_x(x_up),
    )]
    osend[2] = nn(hidden[...], w[x_down]).astype(BF16)
    over_x.append(send(
        osend.at[2, pl.ds(0, mid)], orecv.at[1, pl.ds(0, mid)],
        os_sem.at[3], or_sem.at[3], at_x(x_down),
    ))

    for i, slot in enumerate((x_down, x_up)):
        (cols_down, cols_up)[i].wait_recv()
        to_partner.append(send(
            upr.at[c_me, slot], upr.at[c_me, slot], pfs_sem.at[1 + i], pfr_sem.at[1 + i], partner,
        ))

    oown[...] = nn(hidden[...], w[x_me])
    for h in range(heads):
        attn = ag[:, lanes(h)]
        diffs = jnp.where(mask, nt(attn, v[:, lanes(h)]), 0.0).astype(BF16)
        qg_ref[:, lanes(h)] = (
            nn(diffs, k[:, lanes(h)])
            + jnp.concatenate([nt(attn[span(p)], state_of(0, p, h)) for p in range(2)], axis=0)
        ).astype(BF16)
        kacc[:, lanes(h)] = tn(diffs, q[:, lanes(h)])
        vacc[:, lanes(h)] = tn(wts[h], attn)

    def arrived(into, sem):
        pltpu.make_async_remote_copy(
            src_ref=into, dst_ref=into, send_sem=hs_sem.at[3, 0], recv_sem=sem,
            device_id=partner, device_id_type=MESH,
        ).wait_recv()

    slot = y_down * 2
    arrived(hrow.at[slot], hr_sem.at[0, 0])
    far_row = [send(hrow.at[slot], hrow.at[slot], hs_sem.at[2, 0], hr_sem.at[2, 0], at_row(y_up * 2 + c_me))]
    slot = y_up * 2 + 1
    arrived(hrow.at[slot], hr_sem.at[1, 1])
    far_row.append(
        send(hrow.at[slot], hrow.at[slot], hs_sem.at[2, 1], hr_sem.at[2, 1], at_row(y_down * 2 + c_me))
    )

    for copy in far_y:
        copy.wait_recv()
    to_partner.append(send(
        upr.at[c_me, x_far], upr.at[c_me, x_far], pfs_sem.at[3], pfr_sem.at[3], partner,
    ))

    back2 = row_sums(1, 1, back1)

    out_low.wait_recv()
    osend[1, :mid] = (osend[1, :mid].astype(F32) + orel[0].astype(F32)).astype(BF16)
    over_x.append(send(
        osend.at[1, pl.ds(0, mid)], orecv.at[0, pl.ds(0, mid)],
        os_sem.at[4], or_sem.at[4], at_x(x_up),
    ))
    out_high.wait_recv()
    osend[2, mid:] = (osend[2, mid:].astype(F32) + orel[1].astype(F32)).astype(BF16)
    over_x.append(send(
        osend.at[2, pl.ds(mid, mid)], orecv.at[1, pl.ds(mid, mid)],
        os_sem.at[5], or_sem.at[5], at_x(x_down),
    ))

    arrived(hrow.at[y_down * 2 + 1], hr_sem.at[0, 1])
    arrived(hrow.at[y_up * 2], hr_sem.at[1, 0])
    for copy in far_row + [from_partner] + to_partner:
        copy.wait_recv()
    feats = jnp.concatenate([hrow[r] for r in range(rows)], axis=1)
    def z_at(step):
        return (z_me + step + nz) % nz

    def owner(z, c):
        return (z * rows + y_me * 2 + c, x_me)

    first_x = (z_at(3) // zper)
    for n in range(nx):
        xx = (first_x + n) % nx
        cols = jnp.concatenate(
            [
                jnp.concatenate([upr[r % 2, xx, r // 2, b] for r in range(rows)], axis=1)
                for b in range(zper)
            ],
            axis=0,
        )
        part = nt(cols, feats).astype(BF16)
        for b in range(zper):
            for c in range(2):
                at = b * 128 + c * 64
                wsend[xx * zper + b, c] = part[at:at + 64]
        if n == 1:
            rel_up = send(wsend.at[z_at(3)], wrel.at[0], ws_sem.at[0, 0], wr_sem.at[5, 0], at_z(z_at(1)))
            rel_down = send(wsend.at[z_at(-3)], wrel.at[1], ws_sem.at[0, 1], wr_sem.at[5, 1], at_z(z_at(-1)))
            far_up = send(wsend.at[z_at(4), 0], wfar.at[0], ws_sem.at[1, 0], wr_sem.at[6, 0], at_z(z_at(2)))
            far_down = send(wsend.at[z_at(4), 1], wfar.at[1], ws_sem.at[1, 1], wr_sem.at[6, 1], at_z(z_at(-2)))
    for i, step in enumerate((1, -1)):
        for c in range(2):
            send(
                wsend.at[z_at(step), c], wrow.at[i, c_me],
                ws_sem.at[2 + i, c], wr_sem.at[i, c_me], owner(z_at(step), c),
            )
    swap = send(wsend.at[z_me, 1 - c_me], wrow.at[4, c_me], ws_sem.at[4, 0], wr_sem.at[4, 0], partner)
    wrow[4, c_me] = wsend[z_me, c_me]

    back3 = prefixes(1, 1, back2)

    for i, step in enumerate((2, -2)):
        for copy in ((rel_up, far_up), (rel_down, far_down))[i]:
            copy.wait_recv()
        for c in range(2):
            term = wsend[z_at(step), c].astype(F32) + wrel[i, c].astype(F32)
            if c == i:
                term = term + wfar[i].astype(F32)
            wout[i, c] = term.astype(BF16)
            send(
                wout.at[i, c], wrow.at[2 + i, c_me],
                ws_sem.at[5 + i, c], wr_sem.at[2 + i, c_me], owner(z_at(step), c),
            )

    total = oown[...]
    for copy in over_x:
        copy.wait_recv()
    out_ref[...] = (total + orecv[0].astype(F32) + orecv[1].astype(F32)).astype(BF16)

    given = give_states(1, 1, back3)
    for i in range(heads):
        if i == own:
            given.wait_recv()
        h = (i // own) * own + i % own + c_me * (1 - 2 * (i // own)) * own
        at = tile(h)
        later = [state_of(1, p, h) for p in range(2)]
        kg_ref[:, at] = (
            kacc[:, at]
            + jnp.concatenate([nt(v[span(p), at], later[p]) for p in range(2)], axis=0)
        ).astype(BF16)
        vg_ref[:, at] = (
            vacc[:, at]
            + jnp.concatenate([nn(k[span(p), at], later[p]) for p in range(2)], axis=0)
        ).astype(BF16)

    swap.wait_recv()
    for i in range(4):
        for c in range(2):
            arrived(wrow.at[i, c], wr_sem.at[i, c])
    for c in range(2):
        total = wrow[0, c].astype(F32)
        for i in range(1, 5):
            total = total + wrow[i, c].astype(F32)
        wg_ref[:, c * half:(c + 1) * half] = total
    for copy in waits:
        copy.wait_send()


def write_out(*refs):
    count = len(refs) // 2
    sem = refs[-1]
    copies = [
        pltpu.make_async_copy(refs[i], refs[count + i], sem.at[i]) for i in range(count)
    ]
    for copy in copies:
        copy.start()
    for copy in copies:
        copy.wait()


def on_device(queries, keys, values, out_weight, upstream):
    nx = lax.axis_size("head")
    nz, ny = NZ, NY
    rows = 2 * ny
    pair, length, width = queries.shape
    tokens = pair * length
    heads = width // HEAD_DIM
    dx = upstream.shape[2]
    sl = width // rows
    half = width // 2
    zper = dx // (ny * 128)
    flat = lambda a: a.reshape(tokens, a.shape[2])
    vmem = pltpu.VMEM
    dma = lambda *shape: pltpu.SemaphoreType.DMA(shape)
    part = vmem((2, ny, 2, sl, HEAD_DIM), BF16)
    heads_of = lambda n: vmem((2, n, 2, HEAD_DIM, HEAD_DIM), BF16)
    narrow = vmem((tokens, width), BF16)
    wide = vmem((tokens, width), F32)
    scratch = [
        narrow, narrow, narrow,
        vmem((nx, width, dx), BF16),
        vmem((nx, tokens, dx), BF16),
        vmem((2, ny, zper, 128, tokens), BF16),
        vmem((2, nx, ny, zper, 128, tokens), BF16),
        heads_of(heads), heads_of(heads // 2), part, part,
        vmem((2, 2, sl, HEAD_DIM), BF16),
        vmem((2, nz, sl, HEAD_DIM), BF16),
        part, part, heads_of(heads // 2), heads_of(heads),
        vmem((heads, tokens, tokens), BF16),
        wide, wide, wide, narrow, wide, narrow, wide, wide,
        vmem((width, tokens), BF16), vmem((rows, half, tokens), BF16),
        vmem((nz, 2, 64, half), BF16), vmem((5, 2, 64, half), BF16),
        vmem((2, 2, 64, half), BF16), vmem((2, 64, half), BF16), vmem((2, 2, 64, half), BF16),
        vmem((3, tokens, dx), BF16), vmem((2, tokens // 2, dx), BF16),
        vmem((2, tokens, dx), BF16), vmem((tokens, dx), F32),
        dma(4), dma(nx), dma(2), dma(2), dma(2), dma(2), dma(2, ny), dma(2, ny),
        dma(2), dma(2), dma(4), dma(4),
        dma(2), dma(2), dma(2), dma(2),
        dma(2, ny), dma(2, ny), dma(2, nz), dma(2, nz), dma(2, ny), dma(2, ny),
        dma(4, 2), dma(4, 2), dma(7, 2), dma(7, 2), dma(6), dma(6),
    ]
    grad = jax.ShapeDtypeStruct((tokens, width), BF16)
    shapes = (
        jax.ShapeDtypeStruct((tokens, dx), BF16), grad, grad, grad,
        jax.ShapeDtypeStruct((64, width), F32),
    )
    results = pl.pallas_call(
        functools.partial(kernel, nz, ny, nx),
        out_shape=shapes,
        in_specs=[pl.BlockSpec(memory_space=pltpu.HBM)] * 5,
        out_specs=[pl.BlockSpec(memory_space=pltpu.VMEM)] * 5,
        scratch_shapes=scratch,
        compiler_params=pltpu.CompilerParams(
            collective_id=0, has_side_effects=True, vmem_limit_bytes=48 << 20,
        ),
    )(*[pltpu.with_memory_space_constraint(a, pltpu.HBM) for a in (flat(queries), flat(keys), flat(values), out_weight, flat(upstream))])
    out, qg, kg, vg, wg = pl.pallas_call(
        write_out,
        out_shape=shapes,
        in_specs=[pl.BlockSpec(memory_space=pl.ANY)] * 5,
        out_specs=[pl.BlockSpec(memory_space=pltpu.HBM)] * 5,
        scratch_shapes=[dma(5)],
        compiler_params=pltpu.CompilerParams(vmem_limit_bytes=4 << 20),
    )(*results)
    pairs = lambda a: a.reshape(pair, length, a.shape[1])
    return pairs(out), pairs(qg), pairs(kg), pairs(vg), wg.T


def solution(mesh):
    return jax.shard_map(
        on_device,
        mesh=mesh,
        in_specs=(
            P(None, "seq", "head"),
            P(None, "seq", "head"),
            P(None, "seq", "head"),
            P("head", None),
            P(None, "seq", "head"),
        ),
        out_specs=(
            P(None, "seq", "head"),
            P(None, "seq", "head"),
            P(None, "seq", "head"),
            P(None, "seq", "head"),
            P("head", "seq"),
        ),
        check_vma=False,
    )
```
